256 devices in a mesh: stream: 16 (over x, y_hi, core), shard: 16 (over z, y_lo).
Axes of the slice: x: 4, y: 4 (y_hi: 2, y_lo: 2; y = y_hi * 2 + y_lo), z: 8, core: 2. Of those that a mesh axis runs over, the one named last changes fastest.
Arguments:
- frames_in: bfloat16 [192, 4, 12, 5120], P('stream', None, None, 'shard'), may hold values from -6 to 6
- kept_state: float32 [192, 80, 64, 128], P('stream', 'shard'), may hold values from -6 to 6
- moved_to: int32 [192], P('stream'), may hold values from 0 to 191, as said below
- xz_weight: bfloat16 [5120, 2, 5120], P('stream', None, 'shard'), may hold values from -0.078125 to 0.078125
- side_weight: bfloat16 [5120, 336], P('stream'), may hold values from -0.01953125 to 0.01953125
- xz_mask: int32 [40, 2, 40], replicated, may hold values 0 or 1
- dt_bias: float32 [80], P('shard'), may hold values from -1 to 1
- decay_rate: float32 [80], P('shard'), may hold values from 0.00625 to 0.25
- skip_gain: float32 [80], P('shard'), may hold values from 0.5 to 1.5
- norm_gain: float32 [5120], P('shard'), may hold values from 0.1 to 1.9
- out_weight: bfloat16 [5120, 5120], P('stream', 'shard'), may hold values from -0.078125 to 0.078125
- out_mask: int32 [40, 40], replicated, may hold values 0 or 1
Outputs:
- mixed: bfloat16 [192, 4, 12, 5120], P('stream', None, None, 'shard')
- carry_state: float32 [192, 80, 64, 128], P('stream', 'shard')
The draws below stay inside these ranges and needn't reach their ends.
Inputs may be any that keep to these rules, and one draw needn't show every extreme that they name: `moved_to`: A permutation of the slots; the 12 old slots of index i of stream go, exactly 3 each, to the 4 indices i + 1, i + 2, i + 3 and i + 8 of stream (counted modulo 16).
All inputs are finite; a program needn't handle non-finite values.
Results may differ from the reference program's by a relative error of at most 0.025.
Values may be sent and summed in bfloat16 or wider, within the bound.
A program may use at most 128 MiB of HBM per device.

```python
import math
import jax
import jax.numpy as jnp
from jax import lax

D = 5120
HEADS = 80
HEADDIM = 64
NSTATE = 128
NORM_GROUPS = 16
BLOCK = 128
FRAMES = 4
STREAM_DEV = 12
MOST = 3
PATCH = 12
DINNER = 5120
STREAMS = 192
N_SHARD = 16


def draw_moved_to(key, part):
    device_count = STREAMS // STREAM_DEV
    reach_count = STREAM_DEV // MOST
    first_key, second_key = jax.random.split(key)
    send_order = jax.vmap(lambda sub_key: jax.random.permutation(sub_key, STREAM_DEV))(jax.random.split(first_key, device_count))
    land_order = jax.vmap(lambda sub_key: jax.random.permutation(sub_key, STREAM_DEV))(jax.random.split(second_key, device_count))
    slot_ids = jnp.arange(STREAMS)
    source = slot_ids // STREAM_DEV
    within = slot_ids % STREAM_DEV
    rank_here = send_order[source, within]
    step_index = 1 + rank_here // MOST
    distance = jnp.where(step_index < reach_count, step_index, device_count // 2)
    target = (source + distance) % device_count
    landing_index = (step_index - 1) * MOST + rank_here % MOST
    new_within = land_order[target, landing_index]
    return (target * STREAM_DEV + new_within).astype(jnp.int32)


def place_ends(values, key, least, top_value):
    longest = values.shape.index(max(values.shape))
    spots = []
    for shift in (0, 1):
        where = [jax.random.randint(jax.random.fold_in(key, axis), (), 0, length) for axis, length in enumerate(values.shape)]
        where[longest] = (where[longest] + shift) % values.shape[longest]
        spots.append(tuple(where))
    return values.at[spots[0]].set(least).at[spots[1]].set(top_value)


def shard_levels(stream_key, dims, cuts, least, top_value):
    factor_of, own = 1.0, jax.random.fold_in(stream_key, 6)
    for position, shards_of in cuts:
        heights = jnp.exp(jax.random.uniform(jax.random.fold_in(own, position), (shards_of,), jnp.float32, least / len(cuts), top_value / len(cuts)))
        factor_of = factor_of * jnp.repeat(heights, dims[position] // shards_of).reshape([-1 if axis == position else 1 for axis in range(len(dims))])
    return factor_of


def centred(own_key, dims, deviation, most, shards=(), dtype=jnp.bfloat16):
    values = deviation * jax.random.normal(own_key, dims, jnp.float32)
    if shards:
        values = values * shard_levels(own_key, dims, shards, -0.22, 0.18)
    return jnp.clip(values, -most, most).astype(dtype)


def setup_inputs(seed: int = 0) -> dict:
    seeds = jax.random.split(jax.random.key(seed), 13)
    return {
        "frames_in": centred(seeds[0], (STREAMS, FRAMES, PATCH, D), 1.0, 6.0, ((0, 16), (3, 16))),
        "kept_state": centred(seeds[1], (STREAMS, HEADS, HEADDIM, NSTATE), 1.0, 6.0, ((0, 16), (1, 16)), jnp.float32),
        "moved_to": draw_moved_to(jax.random.fold_in(seeds[12], 71), 0),
        "xz_weight": centred(seeds[3], (D, 2, DINNER), D ** -0.5, 0.078125, ((0, 16), (2, 16))),
        "side_weight": centred(seeds[4], (D, 2 * NSTATE + HEADS), (D * NSTATE // 8) ** -0.5, 0.01953125, ((0, 16),)),
        "xz_mask": place_ends((jax.random.randint(seeds[5], (D // BLOCK, 2, DINNER // BLOCK), 0, 2) < 1).astype(jnp.int32), jax.random.fold_in(seeds[5], 1), 0, 1),
        "dt_bias": jnp.clip(jax.random.uniform(seeds[6], (HEADS,), jnp.float32, -1.0, 1.0) * shard_levels(seeds[6], (HEADS,), ((0, 16),), -0.4, 0.0), -1.0, 1.0),
        "decay_rate": jnp.clip(jnp.exp(math.log(0.25) - 3.6888794 * jax.random.uniform(seeds[7], (HEADS,), jnp.float32) ** shard_levels(seeds[7], (HEADS,), ((0, 16),), -0.2, 0.2)), 0.00625, 0.25),
        "skip_gain": jnp.clip(0.5 + 1.0 * jax.random.uniform(seeds[8], (HEADS,), jnp.float32) ** shard_levels(seeds[8], (HEADS,), ((0, 16),), -0.2, 0.2), 0.5, 1.5),
        "norm_gain": jnp.clip(1.0 + 0.18 * jax.random.normal(seeds[9], (DINNER,), jnp.float32), 0.1, 1.9),
        "out_weight": centred(seeds[10], (D, DINNER), DINNER ** -0.5, 0.078125, ((0, 16), (1, 16))),
        "out_mask": place_ends((jax.random.randint(seeds[11], (D // BLOCK, DINNER // BLOCK), 0, 2) < 1).astype(jnp.int32), jax.random.fold_in(seeds[11], 1), 0, 1),
    }


def frame_step(head_inputs, input_mix, output_mix, step_sizes, decay_rate, skip_gain, carry_state):
    highest = lax.Precision.HIGHEST
    length = head_inputs.shape[1]
    decays = -decay_rate * step_sizes
    cumulative = jnp.cumsum(decays, axis=1)
    causal = (jnp.arange(length)[:, None] >= jnp.arange(length)[None, :])[None, :, :, None]
    between = cumulative[:, :, None, :] - cumulative[:, None, :, :]
    weights = jnp.where(causal, jnp.exp(jnp.where(causal, between, 0.0)), 0.0)
    scores = jnp.einsum('sln,smn->slm', output_mix, input_mix, precision=highest)
    mixing = scores[:, :, :, None] * weights * step_sizes[:, None, :, :]
    inside = jnp.einsum('slmh,smhp->slhp', mixing, head_inputs, precision=highest)
    carried = jnp.exp(cumulative)[:, :, :, None] * jnp.einsum('sln,shpn->slhp', output_mix, carry_state, precision=highest)
    outputs = inside + carried + skip_gain[None, None, :, None] * head_inputs
    to_end = jnp.exp(cumulative[:, -1:, :] - cumulative) * step_sizes
    carry_state = jnp.exp(cumulative[:, -1, :])[:, :, None, None] * carry_state + jnp.einsum('slh,slhp,sln->shpn', to_end, head_inputs, input_mix, precision=highest)
    return (outputs, carry_state)

def reference(frames_in, kept_state, moved_to, xz_weight, side_weight, xz_mask, dt_bias, decay_rate, skip_gain, norm_gain, out_weight, out_mask):
    carry_state = jnp.zeros_like(kept_state).at[moved_to].set(kept_state)
    features = frames_in.reshape(-1, D)
    xz_full = jnp.repeat(jnp.repeat(xz_mask, BLOCK, axis=0), BLOCK, axis=2).astype(jnp.bfloat16)
    xz_total = jnp.dot(features, (xz_weight * xz_full).reshape(D, 2 * DINNER), preferred_element_type=jnp.float32)
    side_total = jnp.dot(features, side_weight, preferred_element_type=jnp.float32)
    head_inputs = xz_total[:, :DINNER].reshape(STREAMS, FRAMES, PATCH, HEADS, HEADDIM)
    gate_inputs = xz_total[:, DINNER:]
    input_mix = side_total[:, :NSTATE].reshape(STREAMS, FRAMES, PATCH, NSTATE)
    output_mix = side_total[:, NSTATE:2 * NSTATE].reshape(STREAMS, FRAMES, PATCH, NSTATE)
    step_sizes = jax.nn.softplus(side_total[:, 2 * NSTATE:] + dt_bias).reshape(STREAMS, FRAMES, PATCH, HEADS)
    results = []
    for frame_index in range(FRAMES):
        outputs, carry_state = frame_step(head_inputs[:, frame_index], input_mix[:, frame_index], output_mix[:, frame_index], step_sizes[:, frame_index], decay_rate, skip_gain, carry_state)
        results.append(outputs)
    row_count = features.shape[0]
    scanned = jnp.stack(results, axis=1).reshape(row_count, DINNER)
    gated = (scanned * jax.nn.silu(gate_inputs)).reshape(row_count, NORM_GROUPS, DINNER // NORM_GROUPS)
    mean_square = lax.optimization_barrier(jnp.mean(gated * gated, axis=2, keepdims=True))
    normed = ((gated * lax.rsqrt(mean_square + 1e-05)).reshape(row_count, DINNER) * norm_gain).astype(jnp.bfloat16)
    out_full = jnp.repeat(jnp.repeat(out_mask, BLOCK, axis=0), BLOCK, axis=1).astype(jnp.bfloat16)
    masked_out = out_weight * out_full
    group_width = DINNER // N_SHARD
    mixed = jnp.zeros((row_count, D), jnp.float32)
    for shard_index in range(N_SHARD):
        low = shard_index * group_width
        partial_term = jnp.dot(normed[:, low:low + group_width], masked_out[:, low:low + group_width].T, preferred_element_type=jnp.float32)
        rounded = lax.optimization_barrier(partial_term.astype(jnp.bfloat16))
        mixed = mixed + rounded.astype(jnp.float32)
    return (mixed.astype(jnp.bfloat16).reshape(STREAMS, FRAMES, PATCH, D), carry_state)
```

```python
import jax
import jax.numpy as jnp
from jax import lax
from jax.experimental import pallas as pl
from jax.experimental.pallas import tpu as pltpu
from jax.sharding import PartitionSpec as P

MESH = pl.DeviceIdType.MESH
F32, BF16 = jnp.float32, jnp.bfloat16
HIGHEST = lax.Precision.HIGHEST

NSTATE = 128
BLOCK = 128
FRAMES = 4
MOST = 3
HOPS = (1, 2, 3, 8)
ROWS = 576
SLOTS = 12
TOKENS = 48
WIDTH = 320
WIDE = 768
GATE_AT = 384
SIDE_AT = 96
MIXES = 32


def place():
    si, ki = lax.axis_index("stream"), lax.axis_index("shard")
    return si // 4, (si // 2) % 2, si % 2, ki // 2, ki % 2


def device(x, y, c, z):
    return {"stream": 4 * x + 2 * (y // 2) + c, "shard": 2 * z + y % 2}


def remote(src, dst, send, recv, where):
    return pltpu.make_async_remote_copy(
        src_ref=src, dst_ref=dst, send_sem=send, recv_sem=recv, device_id=where, device_id_type=MESH
    )


def gather_kernel(
    w1_ref, w2_ref, x_ref, st_ref, sl_ref,
    xz_ref, bc_ref, got_ref, gsl_ref, wo_ref,
    wg, xg, acc, psend, precv, bct, tile,
    ysend, yrecv, xps, xpr, xms, xmr, x2s, x2r, ss, sr,
    zps, zpr, zms, zmr, sts, strv, sls, slr, psn, prc, bcs, bcr,
):
    x, yh, c, z, yl = place()
    y = 2 * yh + yl
    si, ki = lax.axis_index("stream"), lax.axis_index("shard")
    here = 4 * x + y
    xr, xl = (x + 1) % 4, (x + 3) % 4
    half = pl.ds(pl.multiple_of(c * 160, 160), 160)

    barrier = pltpu.get_barrier_semaphore()

    @pl.loop(1, 32)
    def _(i):
        other = (si * 2 + yl + i) % 32
        pl.semaphore_signal(
            barrier, inc=1, device_id={"stream": other // 2, "shard": 2 * z + other % 2}, device_id_type=MESH
        )

    @pl.loop(1, 8)
    def _(i):
        pl.semaphore_signal(
            barrier, inc=1, device_id={"stream": si, "shard": 2 * ((z + i) % 8) + yl}, device_id_type=MESH
        )

    pl.semaphore_wait(barrier, 38)

    pairs = ((w1_ref, wg), (w2_ref, wo_ref))

    def y_copies(w):
        own, full = pairs[w]
        for a in range(2):
            for h in range(2):
                part = pl.ds(h * 160, 160)
                to = c + 2 * a
                mine = (to == y) & (c == h)
                yield mine, remote(
                    own.at[part], full.at[here, part], ysend.at[w, 2 * a + h], yrecv.at[w, y], device(x, to, h, z)
                ), pltpu.make_async_copy(own.at[part], full.at[here, part], yrecv.at[w, y])

    def y_start(w):
        for mine, far, near in y_copies(w):
            @pl.when(mine)
            def _():
                near.start()

            @pl.when(jnp.logical_not(mine))
            def _():
                far.start()

    def y_finish(w):
        for mine, far, near in y_copies(w):
            @pl.when(jnp.logical_not(mine))
            def _():
                far.wait_send()

    def slot(x_of, ys):
        return 4 * x_of + ys

    def hop(w, x_of, ys, send, recv, x_to):
        full = pairs[w][1]
        ref = full.at[slot(x_of, ys), half]
        return remote(ref, ref, send.at[w, ys], recv.at[w, ys], device(x_to, y, c, z))

    def sibling(w, q, x_of, ys):
        full = pairs[w][1]
        ref = full.at[slot(x_of, ys), half]
        return remote(ref, ref, ss.at[w, 4 * q + ys], sr.at[w, 4 * q + ys], device(x, y, 1 - c, z))

    def landed(w, x_of, ys, recv):
        full = pairs[w][1]
        ref = full.at[slot(x_of, ys), half]
        remote(ref, ref, recv.at[w, ys], recv.at[w, ys], device(x, y, 1 - c, z)).wait_recv()

    def stage_x(w, ys):
        full = pairs[w][1]
        ref = full.at[slot(x, ys), half]
        remote(ref, ref, yrecv.at[w, ys], yrecv.at[w, ys], device(x, y, 1 - c, z)).wait_recv()
        hop(w, x, ys, xps, xpr, xr).start()
        hop(w, x, ys, xms, xmr, xl).start()
        sibling(w, 0, x, ys).start()

    def stage_far(w, ys):
        landed(w, xl, ys, xpr)
        if ys < 2:
            hop(w, xl, ys, x2s, x2r, xr).start()
        sibling(w, 1, xl, ys).start()
        landed(w, xr, ys, xmr)
        if ys >= 2:
            hop(w, xr, ys, x2s, x2r, xl).start()
        sibling(w, 2, xr, ys).start()

    def stage_last(w, ys):
        landed(w, (x + 2) % 4, ys, x2r)
        sibling(w, 3, (x + 2) % 4, ys).start()

    def finish(w):
        other = pl.ds(pl.multiple_of((1 - c) * 160, 160), 160)
        full = pairs[w][1]
        y_finish(w)
        for q, x_of in enumerate((x, xl, xr, (x + 2) % 4)):
            for ys in range(4):
                sibling(w, q, x_of, ys).wait_send()
                ref = full.at[slot(x_of, ys), other]
                remote(ref, ref, sr.at[w, 4 * q + ys], sr.at[w, 4 * q + ys], device(x, y, 1 - c, z)).wait_recv()
        for ys in range(4):
            hop(w, x, ys, xps, xpr, xr).wait_send()
            hop(w, x, ys, xms, xmr, xl).wait_send()
            hop(w, xl if ys < 2 else xr, ys, x2s, x2r, xr if ys < 2 else xl).wait_send()

    def ring(t):
        lo = pl.ds(0, 288) if t == 3 else pl.ds(0, ROWS)
        hi = pl.ds(288, 288) if t == 3 else pl.ds(0, ROWS)
        up = xg.at[(z - t + 8) % 8, lo]
        down = xg.at[(z + t) % 8, hi]
        return (
            remote(up, up, zps.at[t], zpr.at[t], {"stream": si, "shard": 2 * ((z + 1) % 8) + yl}),
            remote(down, down, zms.at[t], zmr.at[t], {"stream": si, "shard": 2 * ((z + 7) % 8) + yl}),
        )

    def ring_wait(t):
        lo = pl.ds(0, 288) if t == 3 else pl.ds(0, ROWS)
        hi = pl.ds(288, 288) if t == 3 else pl.ds(0, ROWS)
        up = xg.at[(z - t + 7) % 8, lo]
        down = xg.at[(z + t + 1) % 8, hi]
        remote(up, up, zpr.at[t], zpr.at[t], {"stream": si, "shard": 2 * ((z + 1) % 8) + yl}).wait_recv()
        remote(down, down, zmr.at[t], zmr.at[t], {"stream": si, "shard": 2 * ((z + 1) % 8) + yl}).wait_recv()

    def ring_start(t):
        for copy in ring(t):
            copy.start()

    def states():
        for t, hops in enumerate(HOPS):
            where = {"stream": (si + hops) % 16, "shard": ki}
            yield remote(st_ref.at[pl.ds(MOST * t, MOST)], got_ref.at[pl.ds(MOST * t, MOST)], sts.at[t], strv.at[t], where)
            yield remote(sl_ref.at[t], gsl_ref.at[t], sls.at[t], slr.at[t], where)

    y_start(0)
    xg[z] = x_ref[...]
    ring_start(0)
    stage_x(0, 0)
    stage_x(0, 1)
    stage_x(0, 2)
    stage_x(0, 3)
    ring_wait(0)
    ring_start(1)
    stage_far(0, 0)
    stage_far(0, 1)
    ring_wait(1)
    ring_start(2)
    stage_far(0, 2)
    stage_far(0, 3)
    y_start(1)
    for copy in states():
        copy.start()
    ring_wait(2)
    ring_start(3)
    for ys in range(4):
        stage_last(0, ys)
    ring_wait(3)
    finish(0)
    for ys in range(4):
        stage_x(1, ys)

    def matmul(b, n):
        cols = pl.ds(256 * n, 256)
        acc[...] = jnp.zeros_like(acc)

        @pl.loop(0, 8)
        def _(j):
            acc[...] += jnp.dot(
                xg[j], wg[4 * (j // 2) + 2 * (j % 2) + b, :, cols], preferred_element_type=F32
            )

    partner = {"stream": si, "shard": 2 * z + 1 - yl}

    def swap(n):
        return remote(psend.at[n], precv.at[n], psn.at[n], prc.at[n], partner)

    def mixes(i):
        return remote(
            bct, bc_ref.at[z], bcs.at[i], bcr.at[i], {"stream": si, "shard": 2 * ((z + i + 1) % 8) + yl}
        )

    for step, n in enumerate((1, 0, 2)):
        matmul(1 - yl, n)
        psend[n] = acc[...].astype(BF16)
        swap(n).start()
        if step == 1:
            for ys in range(4):
                stage_far(1, ys)
    for step, n in enumerate((1, 0, 2)):
        matmul(yl, n)
        swap(n).wait()
        total = acc[...] + precv[n].astype(F32)
        xz_ref[:, 256 * n : 256 * (n + 1)] = total
        if step == 0:
            tile[...] = jnp.zeros_like(tile)
            tile[0:ROWS, :] = total[:, 0:128]
            bct[...] = tile[...].T[64 : 64 + MIXES, :].astype(BF16)
            bc_ref[z] = bct[...]
            for i in range(7):
                mixes(i).start()
            for ys in range(4):
                stage_last(1, ys)
    for i in range(7):
        mixes(i).wait_send()
        src = (z + 7 - i) % 8
        remote(bct, bc_ref.at[src], bcr.at[i], bcr.at[i], partner).wait_recv()
    finish(1)
    for t in range(4):
        for copy in ring(t):
            copy.wait_send()
    for copy in states():
        copy.wait()


def gather(w1, w2, xrows, st, sl):
    vmem = pl.BlockSpec(memory_space=pltpu.VMEM)
    dma = pltpu.SemaphoreType.DMA
    return pl.pallas_call(
        gather_kernel,
        out_shape=(
            jax.ShapeDtypeStruct((ROWS, WIDE), F32),
            jax.ShapeDtypeStruct((8, MIXES, 640), BF16),
            jax.ShapeDtypeStruct((SLOTS, WIDTH, NSTATE), BF16),
            jax.ShapeDtypeStruct((4, 8, 128), jnp.int32),
            jax.ShapeDtypeStruct((16, WIDTH, WIDTH), BF16),
        ),
        in_specs=[vmem] * 5,
        out_specs=(vmem,) * 5,
        scratch_shapes=[
            pltpu.VMEM((16, WIDTH, WIDE), BF16),
            pltpu.VMEM((8, ROWS, WIDTH), BF16),
            pltpu.VMEM((ROWS, 256), F32),
            pltpu.VMEM((3, ROWS, 256), BF16),
            pltpu.VMEM((3, ROWS, 256), BF16),
            pltpu.VMEM((MIXES, 640), BF16),
            pltpu.VMEM((640, 128), F32),
        ]
        + [dma((2, 4))] * 8
        + [dma((2, 16))] * 2
        + [dma((4,))] * 8
        + [dma((3,))] * 2
        + [dma((7,))] * 2,
        compiler_params=pltpu.CompilerParams(
            collective_id=0, has_side_effects=True, vmem_limit_bytes=56 * 1024 * 1024
        ),
        name="gather_project",
    )(w1, w2, xrows, st, sl)


def order_kernel(order_ref, in_ref, out_ref):
    out_ref[...] = in_ref[...].astype(BF16)


def order_states(kept, order):
    return pl.pallas_call(
        order_kernel,
        out_shape=jax.ShapeDtypeStruct(kept.shape, BF16),
        grid_spec=pltpu.PrefetchScalarGridSpec(
            num_scalar_prefetch=1,
            grid=(SLOTS,),
            in_specs=[pl.BlockSpec((1, WIDTH, NSTATE), lambda j, order: (order[j], 0, 0))],
            out_specs=pl.BlockSpec((1, WIDTH, NSTATE), lambda j, order: (j, 0, 0)),
        ),
        name="order_states",
    )(order, kept)


def scan_kernel(
    perm_ref, xz_ref, bc_ref, got_ref, head_ref, skip_ref, gain_ref,
    normed_ref, carry_ref,
    mix_in, mix_out, steps,
):
    mix_in[...] = bc_ref[0:4].reshape(NSTATE, 640).astype(F32).T.astype(BF16)
    mix_out[...] = bc_ref[4:8].reshape(NSTATE, 640).astype(F32).T.astype(BF16)
    bias, rate = head_ref[0:1, :], head_ref[1:2, :]
    raw = xz_ref[:, 256:384] + bias
    lane = lax.broadcasted_iota(jnp.int32, (1, 128), 1)
    live = (lane >= SIDE_AT) & (lane < SIDE_AT + 5)
    steps[...] = jnp.where(live, jnp.maximum(raw, 0.0) + jnp.log1p(jnp.exp(-jnp.abs(raw))), 0.0)

    def iota(shape, axis):
        return lax.broadcasted_iota(jnp.int32, shape, axis)

    spread = (iota((128, WIDTH), 0) == SIDE_AT + iota((128, WIDTH), 1) // 64).astype(F32)
    spread_tokens = (iota((128, 240), 0) == SIDE_AT + iota((128, 240), 1) // TOKENS).astype(F32)
    lower = (iota((TOKENS, TOKENS), 0) >= iota((TOKENS, TOKENS), 1)).astype(F32)
    token_of = iota((TOKENS, 240), 1) % TOKENS
    causal = iota((TOKENS, 240), 0) >= token_of
    same = iota((TOKENS, 240), 0) == token_of
    head_of = iota((TOKENS, WIDTH), 1) // 64
    ones = jnp.ones((8, NSTATE), F32)
    skip, gain = skip_ref[...], gain_ref[...]

    def dot(a, b, dims, precision=None):
        return lax.dot_general(a, b, (dims, ((), ())), preferred_element_type=F32, precision=precision)

    nt, nn, tn = ((1,), (1,)), ((1,), (0,)), ((0,), (0,))

    @pl.loop(0, SLOTS)
    def _(s):
        rows = pl.ds(pl.multiple_of(s * TOKENS, TOKENS), TOKENS)
        step = steps[rows, :]
        cumulative = dot(lower, -rate * step, nn, HIGHEST)
        cum_wide = dot(cumulative, spread, nn, HIGHEST)
        step_wide = dot(step, spread, nn, HIGHEST)
        cum_left = dot(cumulative, spread_tokens, nn, HIGHEST)
        cum_right = jnp.sum(jnp.where(same, cum_left, 0.0), axis=0, keepdims=True)
        b_s, c_s = mix_in[rows, :], mix_out[rows, :]
        scores = dot(c_s, jnp.concatenate([b_s] * 5, axis=0), nt)
        mixing = jnp.where(causal, jnp.exp(jnp.where(causal, cum_left - cum_right, 0.0)) * scores, 0.0).astype(BF16)
        inputs = xz_ref[rows, 0:WIDTH]
        stepped = inputs * step_wide
        stepped_b = stepped.astype(BF16)
        blocks = jnp.concatenate(
            [jnp.where(head_of == h, stepped_b, jnp.zeros_like(stepped_b)) for h in range(5)], axis=0
        )
        state = got_ref[perm_ref[s]]
        out = dot(mixing, blocks, nn)
        out += jnp.exp(cum_wide) * dot(c_s, state, nt)
        out += skip * inputs
        last = cum_wide[TOKENS - 1 : TOKENS, :]
        to_end = (jnp.exp(last - cum_wide) * stepped).astype(BF16)
        fade = jnp.where(iota((8, WIDTH), 0) == 0, jnp.exp(last), 0.0)
        carry_ref[s] = dot(fade, ones, tn, HIGHEST) * state.astype(F32) + dot(to_end, b_s, tn)
        gate = xz_ref[rows, GATE_AT : GATE_AT + WIDTH]
        gated = out * gate * (1.0 / (1.0 + jnp.exp(-gate)))
        mean_square = jnp.sum(gated * gated, axis=1, keepdims=True) * (1.0 / WIDTH)
        normed_ref[rows, :] = (gated * lax.rsqrt(mean_square + 1e-05) * gain).astype(BF16)


def scan_frames(perm, xz, bc, got, head, skip, gain):
    vmem = pl.BlockSpec(memory_space=pltpu.VMEM)
    return pl.pallas_call(
        scan_kernel,
        out_shape=(
            jax.ShapeDtypeStruct((ROWS, WIDTH), BF16),
            jax.ShapeDtypeStruct((SLOTS, WIDTH, NSTATE), F32),
        ),
        in_specs=[pl.BlockSpec(memory_space=pltpu.SMEM)] + [vmem] * 6,
        out_specs=(vmem, vmem),
        scratch_shapes=[
            pltpu.VMEM((640, NSTATE), BF16),
            pltpu.VMEM((640, NSTATE), BF16),
            pltpu.VMEM((ROWS, 128), F32),
        ],
        compiler_params=pltpu.CompilerParams(vmem_limit_bytes=32 * 1024 * 1024),
        name="scan_norm",
    )(perm, xz, bc, got, head, skip, gain)


def reduce_kernel(
    normed_ref, wo_ref, mixed_ref,
    both, sendp, recvp, sendm, recvm,
    ns, nr, ps, pr, ms, mr,
):
    x, yh, c, z, yl = place()
    si = lax.axis_index("stream")
    up = {"stream": si, "shard": 2 * ((z + 1) % 8) + yl}
    down = {"stream": si, "shard": 2 * ((z + 7) % 8) + yl}
    partner = {"stream": si, "shard": 2 * z + 1 - yl}
    barrier = pltpu.get_barrier_semaphore()
    for where in (up, down, partner):
        pl.semaphore_signal(barrier, inc=1, device_id=where, device_id_type=MESH)
    pl.semaphore_wait(barrier, 3)

    def rows(q):
        return pl.ds(288 * q, 288)

    def give(q):
        return remote(normed_ref.at[rows(q)], both.at[yl, rows(q)], ns.at[q], nr.at[q], partner)

    def get(q):
        return remote(normed_ref.at[rows(q)], both.at[1 - yl, rows(q)], ns.at[q], nr.at[q], partner)

    give(0).start()
    give(1).start()
    both[yl] = normed_ref[...]

    def term(to, q):
        at = 4 * (to // 2) + 2 * (to % 2)
        total = None
        for b in range(2):
            one = lax.dot_general(
                both[b, rows(q), :], wo_ref[at + b], (((1,), (1,)), ((), ())), preferred_element_type=F32
            )
            total = one if total is None else total + one
        return total

    def ring(sign, t, q):
        if sign > 0:
            return remote(sendp.at[t, rows(q)], recvp.at[t, rows(q)], ps.at[t, q], pr.at[t, q], up)
        return remote(sendm.at[t, rows(q)], recvm.at[t, rows(q)], ms.at[t, q], mr.at[t, q], down)

    def go(sign, t, q):
        first = t == 0 or (t == 1 and q == (1 if sign > 0 else 0))
        value = term((z + 8 + sign * (4 - t)) % 8, q)
        send, recv = (sendp, recvp) if sign > 0 else (sendm, recvm)
        if not first:
            ring(sign, t - 1, q).wait_recv()
            value = value + recv[t - 1, rows(q), :].astype(F32)
        send[t, rows(q), :] = value.astype(BF16)
        ring(sign, t, q).start()

    get(0).wait_recv()
    go(1, 0, 0)
    go(-1, 1, 0)
    get(1).wait_recv()
    go(-1, 0, 1)
    go(1, 1, 1)
    go(1, 1, 0)
    go(-1, 1, 1)
    go(-1, 2, 0)
    go(1, 2, 1)
    go(1, 2, 0)
    go(-1, 2, 1)
    go(-1, 3, 0)
    go(1, 3, 1)
    go(1, 3, 0)
    go(-1, 3, 1)
    for q in range(2):
        value = term(z, q)
        ring(1, 3, q).wait_recv()
        ring(-1, 3, q).wait_recv()
        value = value + recvp[3, rows(q), :].astype(F32) + recvm[3, rows(q), :].astype(F32)
        mixed_ref[rows(q), :] = value.astype(BF16)
    for q in range(2):
        give(q).wait_send()
        for t in range(4):
            if not (t == 0 and q == 1):
                ring(1, t, q).wait_send()
            if not (t == 0 and q == 0):
                ring(-1, t, q).wait_send()


def project_reduce(normed, wo):
    vmem = pl.BlockSpec(memory_space=pltpu.VMEM)
    dma = pltpu.SemaphoreType.DMA
    return pl.pallas_call(
        reduce_kernel,
        out_shape=jax.ShapeDtypeStruct((ROWS, WIDTH), BF16),
        in_specs=[vmem, vmem],
        out_specs=vmem,
        scratch_shapes=[pltpu.VMEM((2, ROWS, WIDTH), BF16)]
        + [pltpu.VMEM((4, ROWS, WIDTH), BF16)] * 4
        + [dma((2,))] * 2
        + [dma((4, 2))] * 4,
        compiler_params=pltpu.CompilerParams(
            collective_id=1, has_side_effects=True, vmem_limit_bytes=40 * 1024 * 1024
        ),
        name="project_reduce",
    )(normed, wo)


def on_device(
    frames_in,
    kept_state,
    moved_to,
    xz_weight,
    side_weight,
    xz_mask,
    dt_bias,
    decay_rate,
    skip_gain,
    norm_gain,
    out_weight,
    out_mask,
):
    si, ki = lax.axis_index("stream"), lax.axis_index("shard")
    z = ki // 2
    target = moved_to // SLOTS
    distance = (target - si + 16) % 16
    way = jnp.minimum(distance - 1, 3)
    ids = jnp.arange(SLOTS)
    rank = jnp.sum((way[:, None] == way[None, :]) & (ids[:, None] > ids[None, :]), axis=1)
    position = way * MOST + rank
    chosen = position[:, None] == ids[None, :]
    order = jnp.sum(jnp.where(chosen, ids[:, None], 0), axis=0).astype(jnp.int32)
    sent_slots = jnp.sum(jnp.where(chosen, (moved_to % SLOTS)[:, None], 0), axis=0).astype(jnp.int32)
    sl = jnp.broadcast_to(jnp.pad(sent_slots.reshape(4, 1, MOST), ((0, 0), (0, 0), (0, 128 - MOST))), (4, 8, 128))
    st = order_states(kept_state.reshape(SLOTS, WIDTH, NSTATE), order)

    rows_of = ((si * WIDTH + jnp.arange(WIDTH)) // BLOCK)[:, None] == jnp.arange(40)[None, :]
    cols_of = jnp.arange(40)[:, None] == ((ki * WIDTH + jnp.arange(WIDTH)) // BLOCK)[None, :]
    masks = jnp.concatenate([xz_mask.reshape(40, 80), out_mask], axis=1).astype(BF16)
    by_row = jnp.dot(rows_of.astype(BF16), masks)
    cols_b = cols_of.astype(BF16)
    keep = [jnp.dot(by_row[:, 40 * g : 40 * (g + 1)], cols_b) for g in range(3)]
    mixes = lax.dynamic_slice_in_dim(side_weight, MIXES * z, MIXES, 1)
    step_cols = lax.dynamic_slice_in_dim(side_weight, 2 * NSTATE + 5 * ki, 5, 1)
    w1 = jnp.concatenate(
        [
            xz_weight[:, 0, :] * keep[0],
            mixes,
            step_cols,
            jnp.zeros((WIDTH, 27), BF16),
            xz_weight[:, 1, :] * keep[1],
            jnp.zeros((WIDTH, 64), BF16),
        ],
        axis=1,
    )
    w2 = out_weight * keep[2]

    xz, bc, got, gsl, wo = gather(w1, w2, frames_in.reshape(ROWS, WIDTH), st, sl)

    got_slots = gsl[:, 0, :MOST].reshape(SLOTS)
    perm = jnp.sum(jnp.where(got_slots[:, None] == ids[None, :], ids[:, None], 0), axis=0).astype(jnp.int32)
    head = jnp.pad(jnp.stack([dt_bias, decay_rate]), ((0, 6), (SIDE_AT, 128 - SIDE_AT - 5)))
    skip = jnp.repeat(skip_gain, 64).reshape(1, WIDTH)
    normed, carry = scan_frames(perm, xz, bc, got, head, skip, norm_gain.reshape(1, WIDTH))
    mixed = project_reduce(normed, wo)
    return (
        mixed.reshape(SLOTS, FRAMES, TOKENS // FRAMES, WIDTH),
        carry.reshape(SLOTS, 5, 64, NSTATE),
    )


def solution(mesh):
    placed = (
        P("stream", None, None, "shard"),
        P("stream", "shard", None, None),
        P("stream"),
        P("stream", None, "shard"),
        P("stream", None),
        P(),
        P("shard"),
        P("shard"),
        P("shard"),
        P("shard"),
        P("stream", "shard"),
        P(),
    )
    return jax.shard_map(
        on_device,
        mesh=mesh,
        in_specs=placed,
        out_specs=(P("stream", None, None, "shard"), P("stream", "shard", None, None)),
        check_vma=False,
    )
```

```python
import jax
import jax.numpy as jnp
from jax import lax
from jax.experimental import pallas as pl
from jax.experimental.pallas import tpu as pltpu
from jax.sharding import PartitionSpec as P

MESH = pl.DeviceIdType.MESH
F32, BF16 = jnp.float32, jnp.bfloat16

NSTATE = 128
BLOCK = 128
FRAMES = 4
MOST = 3
HOPS = (1, 2, 3, 8)
ROWS = 576
SLOTS = 12
TOKENS = 48
WIDTH = 320
WIDE = 768
GATE_AT = 384
SIDE_AT = 96
MIXES = 32
QUARTER = 144
NT, NN, TN = ((1,), (1,)), ((1,), (0,)), ((0,), (0,))


def place():
    si, ki = lax.axis_index("stream"), lax.axis_index("shard")
    return si // 4, (si // 2) % 2, si % 2, ki // 2, ki % 2


def device(x, y, c, z):
    return {"stream": 4 * x + 2 * (y // 2) + c, "shard": 2 * z + y % 2}


def remote(src, dst, send, recv, where):
    return pltpu.make_async_remote_copy(
        src_ref=src, dst_ref=dst, send_sem=send, recv_sem=recv, device_id=where, device_id_type=MESH
    )


def dot(a, b, dims):
    return lax.dot_general(a, b, (dims, ((), ())), preferred_element_type=F32)


def iota(shape, axis):
    return lax.broadcasted_iota(jnp.int32, shape, axis)


def halves(value):
    high = value.astype(BF16)
    return high, (value - high.astype(F32)).astype(BF16)


def layer_kernel(
    moved_ref, bias_ref, rate_ref, skip_ref,
    wx_ref, wgate_ref, wout_ref, side_ref, xmask_ref, omask_ref, x_ref, kept_ref, gain_ref,
    mixed_ref, carry_ref,
    w1, w2, wg, wo, wrem, xm, xr, xk, st, sl, got, gsl, gsl_s, perm,
    xz, psend, precv, bct, bc, tile, mix_in, mix_out, steps,
    both, sendp, recvp, sendm, recvm,
    ysend, yrecv, xps, xpr, xms, xmr, x2s, x2r, ss, sr,
    zps, zpr, zms, zmr, sts, strv, sls, slr, psn, prc, bcs, bcr,
    ns, nr, ps, pr, ms, mr, local,
):
    x, yh, c, z, yl = place()
    y = 2 * yh + yl
    si, ki = lax.axis_index("stream"), lax.axis_index("shard")
    here = 4 * x + y
    xrt, xlt = (x + 1) % 4, (x + 3) % 4
    half = pl.ds(pl.multiple_of(c * 160, 160), 160)
    up = {"stream": si, "shard": 2 * ((z + 1) % 8) + yl}
    down = {"stream": si, "shard": 2 * ((z + 7) % 8) + yl}
    partner = {"stream": si, "shard": 2 * z + 1 - yl}
    peer = device(x, y, 1 - c, z)

    barrier = pltpu.get_barrier_semaphore()

    @pl.loop(1, 32)
    def _(i):
        other = (si * 2 + yl + i) % 32
        pl.semaphore_signal(
            barrier, inc=1, device_id={"stream": other // 2, "shard": 2 * z + other % 2}, device_id_type=MESH
        )

    @pl.loop(1, 8)
    def _(i):
        pl.semaphore_signal(
            barrier, inc=1, device_id={"stream": si, "shard": 2 * ((z + i) % 8) + yl}, device_id_type=MESH
        )

    xm[z] = x_ref[:, 0:256]
    xr[z] = jnp.concatenate([x_ref[0:288, 256:320], x_ref[288:576, 256:320]], axis=1)

    rows_of = (iota((WIDTH, 40), 1) == (si * WIDTH + iota((WIDTH, 40), 0)) // BLOCK).astype(BF16)
    cols_of = (iota((40, WIDTH), 0) == (ki * WIDTH + iota((40, WIDTH), 1)) // BLOCK).astype(BF16)

    def keep(mask):
        return dot(dot(rows_of, mask.astype(F32).astype(BF16), NN).astype(BF16), cols_of, NN).astype(BF16)

    pick = iota((336, 64), 1)
    pick_row = iota((336, 64), 0)
    chosen = jnp.where(pick < MIXES, pick + MIXES * z, pick - MIXES + 2 * NSTATE + 5 * ki)
    chosen = (pick_row == chosen) & (pick < MIXES + 5)
    side = dot(side_ref[...], chosen.astype(F32).astype(BF16), NN).astype(BF16)
    w1[:, 0:WIDTH] = wx_ref[...] * keep(xmask_ref[0])
    w1[:, WIDTH : WIDTH + 64] = side
    w1[:, GATE_AT : GATE_AT + WIDTH] = wgate_ref[...] * keep(xmask_ref[1])
    w1[:, GATE_AT + WIDTH : WIDE] = jnp.zeros((WIDTH, 64), BF16)

    pl.semaphore_wait(barrier, 38)

    pairs = ((w1, wg), (w2, wo))

    def y_copies(w):
        own, full = pairs[w]
        for a in range(2):
            for h in range(2):
                part = pl.ds(h * 160, 160)
                to = c + 2 * a
                mine = (to == y) & (c == h)
                yield mine, remote(
                    own.at[part], full.at[here, part], ysend.at[w, 2 * a + h], yrecv.at[w, y], device(x, to, h, z)
                ), pltpu.make_async_copy(own.at[part], full.at[here, part], yrecv.at[w, y])

    def y_start(w):
        for mine, far, near in y_copies(w):
            @pl.when(mine)
            def _():
                near.start()

            @pl.when(jnp.logical_not(mine))
            def _():
                far.start()

    def y_finish(w):
        for mine, far, near in y_copies(w):
            @pl.when(jnp.logical_not(mine))
            def _():
                far.wait_send()

    def block(w, x_of, ys, part=half):
        return pairs[w][1].at[4 * x_of + ys, part]

    def hop(w, x_of, ys, send, recv, x_to):
        ref = block(w, x_of, ys)
        return remote(ref, ref, send.at[w, ys], recv.at[w, ys], device(x_to, y, c, z))

    def sibling(w, q, x_of, ys):
        ref = block(w, x_of, ys)
        return remote(ref, ref, ss.at[w, 4 * q + ys], sr.at[w, 4 * q + ys], peer)

    def landed(w, x_of, ys, recv):
        ref = block(w, x_of, ys)
        remote(ref, ref, recv.at[w, ys], recv.at[w, ys], peer).wait_recv()

    def stage_x(w, ys):
        landed(w, x, ys, yrecv)
        hop(w, x, ys, xps, xpr, xrt).start()
        hop(w, x, ys, xms, xmr, xlt).start()
        sibling(w, 0, x, ys).start()

    def stage_far(w, ys):
        landed(w, xlt, ys, xpr)
        if ys < 2:
            hop(w, xlt, ys, x2s, x2r, xrt).start()
        sibling(w, 1, xlt, ys).start()
        landed(w, xrt, ys, xmr)
        if ys >= 2:
            hop(w, xrt, ys, x2s, x2r, xlt).start()
        sibling(w, 2, xrt, ys).start()

    def stage_last(w, ys):
        landed(w, (x + 2) % 4, ys, x2r)
        sibling(w, 3, (x + 2) % 4, ys).start()

    def finish(w):
        other = pl.ds(pl.multiple_of((1 - c) * 160, 160), 160)
        y_finish(w)
        for q, x_of in enumerate((x, xlt, xrt, (x + 2) % 4)):
            for ys in range(4):
                sibling(w, q, x_of, ys).wait_send()
                ref = block(w, x_of, ys, other)
                remote(ref, ref, sr.at[w, 4 * q + ys], sr.at[w, 4 * q + ys], peer).wait_recv()
        for ys in range(4):
            hop(w, x, ys, xps, xpr, xrt).wait_send()
            hop(w, x, ys, xms, xmr, xlt).wait_send()
            hop(w, xlt if ys < 2 else xrt, ys, x2s, x2r, xrt if ys < 2 else xlt).wait_send()

    def piece(t, sign, g, src):
        if g == 2:
            part = pl.ds(0, 288) if t < 3 else pl.ds(0 if sign > 0 else 144, 144)
            return xr.at[src, part]
        if t < 3:
            return xm.at[src, pl.ds(288 * g, 288)]
        return xm.at[src, pl.ds((0 if sign > 0 else 288) + 144 * g, 144)]

    def ring(t, sign, g):
        ref = piece(t, sign, g, (z - sign * t + 8) % 8)
        if sign > 0:
            return remote(ref, ref, zps.at[t, g], zpr.at[t, g], up)
        return remote(ref, ref, zms.at[t, g], zmr.at[t, g], down)

    def ring_start(t):
        for g in range(3):
            for sign in (1, -1):
                if 0 < t < 3:
                    ring_land(t - 1, sign, g)
                ring(t, sign, g).start()

    def ring_land(t, sign, g):
        ref = piece(t, sign, g, (z - sign * (t + 1) + 8) % 8)
        sem = zpr if sign > 0 else zmr
        remote(ref, ref, sem.at[t, g], sem.at[t, g], up).wait_recv()

    def states():
        for t, hops in enumerate(HOPS):
            where = {"stream": (si + hops) % 16, "shard": ki}
            yield remote(st.at[pl.ds(MOST * t, MOST)], got.at[pl.ds(MOST * t, MOST)], sts.at[t], strv.at[t], where)
            yield remote(sl, gsl.at[t], sls.at[t], slr.at[t], where)

    y_start(0)
    ring_start(0)
    w2[...] = wout_ref[...] * keep(omask_ref[...])
    stage_x(0, 0)
    stage_x(0, 1)

    ways = [jnp.minimum((moved_ref[j] // SLOTS - si + 16) % 16 - 1, 3) for j in range(SLOTS)]
    spots = []
    for j in range(SLOTS):
        rank = sum(((ways[i] == ways[j]).astype(jnp.int32) for i in range(j)), jnp.int32(0))
        spots.append(MOST * ways[j] + rank)
    lane = iota((8, 128), 1)
    slots = jnp.zeros((8, 128), jnp.int32)
    for j in range(SLOTS):
        slots = jnp.where(lane == spots[j], moved_ref[j] % SLOTS, slots)
    sl[...] = slots
    stage_x(0, 2)
    stage_x(0, 3)
    for p in range(SLOTS):
        source = sum((jnp.where(spots[j] == p, j, 0) for j in range(1, SLOTS)), jnp.int32(0))
        st[p] = kept_ref[jnp.minimum(source, SLOTS - 1)].astype(BF16)
    ring_start(1)
    stage_far(0, 0)
    stage_far(0, 1)
    ring_start(2)
    stage_far(0, 2)
    stage_far(0, 3)
    y_start(1)
    for copy in states():
        copy.start()
    for g in range(3):
        for sign in (1, -1):
            ring_land(2, sign, g)
    ring_start(3)
    for ys in range(4):
        stage_last(0, ys)
    for g in range(3):
        for sign in (1, -1):
            ring_land(3, sign, g)

    low = iota((288, 128), 1) < 64
    for i in range(4):
        first, second = xr[2 * i].astype(F32), xr[2 * i + 1].astype(F32)
        lanes = slice(128 * (i % 2), 128 * (i % 2) + 128)
        xk[i // 2, 0:288, lanes] = jnp.where(low, first, pltpu.roll(second, 64, 1)).astype(BF16)
        xk[i // 2, 288:576, lanes] = jnp.where(low, pltpu.roll(first, 64, 1), second).astype(BF16)
    finish(0)
    for j in range(8):
        for b in range(2):
            wrem[b, 64 * j : 64 * j + 64, :] = wg[4 * (j // 2) + 2 * (j % 2) + b, 256:320, :]
    for ys in range(4):
        stage_x(1, ys)

    def matmul(b, n, r):
        cols = slice(256 * n, 256 * n + 256)
        rows = slice(288 * r, 288 * r + 288)
        total = None
        for j in range(8):
            one = dot(xm[j, rows, :], wg[4 * (j // 2) + 2 * (j % 2) + b, 0:256, cols], NN)
            total = one if total is None else total + one
        for i in range(2):
            total = total + dot(xk[i, rows, :], wrem[b, 256 * i : 256 * i + 256, cols], NN)
        return total

    def swap(n, r):
        rows = pl.ds(288 * r, 288)
        return remote(psend.at[n, rows], precv.at[n, rows], psn.at[n, r], prc.at[n, r], partner)

    def mixes(i):
        return remote(bct, bc.at[z], bcs.at[i], bcr.at[i], {"stream": si, "shard": 2 * ((z + i + 1) % 8) + yl})

    order = ((1, 0), (1, 1), (0, 0), (2, 0), (0, 1), (2, 1))
    for n, r in order:
        psend[n, 288 * r : 288 * r + 288, :] = matmul(1 - yl, n, r).astype(BF16)
        swap(n, r).start()

    def own(n, r):
        rows = slice(288 * r, 288 * r + 288)
        total = matmul(yl, n, r)
        swap(n, r).wait_recv()
        xz[rows, 256 * n : 256 * n + 256] = total + precv[n, rows, :].astype(F32)

    own(1, 0)
    own(1, 1)
    tile[ROWS:640, :] = jnp.zeros((640 - ROWS, 128), F32)
    tile[0:ROWS, :] = xz[:, 256:384]
    bct[...] = tile[...].T[64 : 64 + MIXES, :].astype(BF16)
    bc[z] = bct[...]
    for i in range(7):
        mixes(i).start()
    for ys in range(4):
        stage_far(1, ys)
    own(0, 0)
    own(2, 0)

    for copy in states():
        copy.wait()
    fetch = pltpu.make_async_copy(gsl, gsl_s, local)
    fetch.start()
    raw_bias = jnp.zeros((1, 128), F32)
    rate = jnp.zeros((1, 128), F32)
    skip = jnp.zeros((1, WIDTH), F32)
    for h in range(5):
        raw_bias = jnp.where(iota((1, 128), 1) == SIDE_AT + h, bias_ref[h], raw_bias)
        rate = jnp.where(iota((1, 128), 1) == SIDE_AT + h, rate_ref[h], rate)
        skip = jnp.where(iota((1, WIDTH), 1) // 64 == h, skip_ref[h], skip)
    gain = gain_ref[...]
    raw = xz[:, 256:384] + raw_bias
    live = (iota((1, 128), 1) >= SIDE_AT) & (iota((1, 128), 1) < SIDE_AT + 5)
    steps[...] = jnp.where(live, jnp.maximum(raw, 0.0) + jnp.log1p(jnp.exp(-jnp.abs(raw))), 0.0)
    fetch.wait()
    landing = [gsl_s[j // MOST, 0, j] for j in range(SLOTS)]
    for s in range(SLOTS):
        found = sum((jnp.where(landing[j] == s, j, 0) for j in range(1, SLOTS)), jnp.int32(0))
        perm[s] = jnp.minimum(found, SLOTS - 1)

    for i in range(7):
        src = (z + 7 - i) % 8
        remote(bct, bc.at[src], bcr.at[i], bcr.at[i], partner).wait_recv()
    mix_in[...] = bc[0:4].reshape(NSTATE, 640).astype(F32).T.astype(BF16)
    mix_out[...] = bc[4:8].reshape(NSTATE, 640).astype(F32).T.astype(BF16)

    spread = jnp.concatenate(
        [
            iota((128, 384), 0) == SIDE_AT + iota((128, 384), 1) // 64,
            (iota((128, 256), 0) == SIDE_AT + iota((128, 256), 1) // TOKENS) & (iota((128, 256), 1) < 240),
        ],
        axis=1,
    ).astype(F32).astype(BF16)
    spread = jnp.concatenate([spread, spread], axis=0)
    in_order = iota((TOKENS, TOKENS), 0) >= iota((TOKENS, TOKENS), 1)
    lower = in_order.astype(F32).astype(BF16)
    token_of = iota((TOKENS, 240), 1) % TOKENS
    causal = iota((TOKENS, 240), 0) >= token_of
    same = iota((TOKENS, 240), 0) == token_of
    head_of = iota((TOKENS, WIDTH), 1) // 64
    ones = jnp.ones((16, NSTATE), BF16)

    def scan(q):
        @pl.loop(0, 3)
        def _(i):
            s = 3 * q + i
            rows = pl.ds(pl.multiple_of(s * TOKENS, TOKENS), TOKENS)
            step = steps[rows, :]
            step_parts = halves(step)
            decay_parts = halves(-rate * step)
            cumulative = dot(lower, decay_parts[0], NN) + dot(lower, decay_parts[1], NN)
            cum_all = dot(jnp.concatenate(halves(cumulative), axis=1), spread, NN)
            step_wide = dot(jnp.concatenate(step_parts, axis=1), spread[:, 0:384], NN)[:, 0:WIDTH]
            cum_wide = cum_all[:, 0:WIDTH]
            cum_left = cum_all[:, 384:624]
            cum_right = jnp.sum(jnp.where(same, cum_left, 0.0), axis=0, keepdims=True)
            b_s, c_s = mix_in[rows, :], mix_out[rows, :]
            scores = dot(c_s, jnp.concatenate([b_s] * 5, axis=0), NT)
            mixing = jnp.where(causal, jnp.exp(jnp.where(causal, cum_left - cum_right, 0.0)) * scores, 0.0).astype(BF16)
            inputs = xz[rows, 0:WIDTH]
            stepped = inputs * step_wide
            stepped_b = stepped.astype(BF16)
            blocks = jnp.concatenate(
                [jnp.where(head_of == h, stepped_b, jnp.zeros_like(stepped_b)) for h in range(5)], axis=0
            )
            state = got[perm[s]]
            out = dot(mixing, blocks, NN)
            out += jnp.exp(cum_wide) * dot(c_s, state, NT)
            out += skip * inputs
            last = cum_wide[TOKENS - 1 : TOKENS, :]
            to_end = (jnp.exp(last - cum_wide) * stepped).astype(BF16)
            fade_high, fade_low = halves(jnp.exp(last))
            first = iota((16, WIDTH), 0)
            zero = jnp.zeros((16, WIDTH), BF16)
            fade = jnp.where(first == 0, fade_high, jnp.where(first == 1, fade_low, zero))
            carry_ref[s] = dot(fade, ones, TN) * state.astype(F32) + dot(to_end, b_s, TN)
            gate = xz[rows, GATE_AT : GATE_AT + WIDTH]
            gated = out * gate * (1.0 / (1.0 + jnp.exp(-gate)))
            mean_square = jnp.sum(gated * gated, axis=1, keepdims=True) * (1.0 / WIDTH)
            both[yl, rows, :] = (gated * lax.rsqrt(mean_square + 1e-05) * gain).astype(BF16)

    def rows_at(q):
        return pl.ds(QUARTER * q, QUARTER)

    def give(q):
        ref = both.at[yl, rows_at(q)]
        return remote(ref, ref, ns.at[q], nr.at[q], partner)

    def given(q):
        ref = both.at[1 - yl, rows_at(q)]
        remote(ref, ref, nr.at[q], nr.at[q], partner).wait_recv()

    def term(to, q):
        at = 4 * (to // 2) + 2 * (to % 2)
        return dot(both[0, rows_at(q), :], wo[at], NT) + dot(both[1, rows_at(q), :], wo[at + 1], NT)

    def relay(sign, t, q):
        if sign > 0:
            return remote(sendp.at[t, rows_at(q)], recvp.at[t, rows_at(q)], ps.at[t, q], pr.at[t, q], up)
        return remote(sendm.at[t, rows_at(q)], recvm.at[t, rows_at(q)], ms.at[t, q], mr.at[t, q], down)

    def starts(sign, q):
        return 0 if (q < 2) == (sign > 0) else 1

    def go(t, q):
        for sign in (1, -1):
            if t < starts(sign, q):
                continue
            value = term((z + 8 + sign * (4 - t)) % 8, q)
            send, recv = (sendp, recvp) if sign > 0 else (sendm, recvm)
            if t > starts(sign, q):
                relay(sign, t - 1, q).wait_recv()
                value = value + recv[t - 1, rows_at(q), :].astype(F32)
            send[t, rows_at(q), :] = value.astype(BF16)
            relay(sign, t, q).start()

    def arrive(q):
        value = term(z, q)
        relay(1, 3, q).wait_recv()
        relay(-1, 3, q).wait_recv()
        value = value + recvp[3, rows_at(q), :].astype(F32) + recvm[3, rows_at(q), :].astype(F32)
        mixed_ref[rows_at(q), :] = value.astype(BF16)

    scan(0)
    give(0).start()
    scan(1)
    give(1).start()
    for ys in range(4):
        stage_last(1, ys)
    own(0, 1)
    own(2, 1)
    finish(1)
    given(0)
    go(0, 0)
    scan(2)
    give(2).start()
    given(1)
    go(0, 1)
    go(1, 0)
    scan(3)
    give(3).start()
    go(1, 1)
    given(2)
    go(0, 2)
    go(2, 0)
    given(3)
    go(0, 3)
    go(1, 2)
    go(2, 1)
    go(3, 0)
    go(1, 3)
    go(2, 2)
    go(3, 1)
    go(2, 3)
    arrive(0)
    go(3, 2)
    arrive(1)
    go(3, 3)
    arrive(2)
    arrive(3)

    for q in range(4):
        give(q).wait_send()
        for sign in (1, -1):
            for t in range(starts(sign, q), 4):
                relay(sign, t, q).wait_send()
    for n, r in order:
        swap(n, r).wait_send()
    for i in range(7):
        mixes(i).wait_send()
    for t in range(4):
        for g in range(3):
            ring(t, 1, g).wait_send()
            ring(t, -1, g).wait_send()


def layer(moved, bias, rate, skip, wx, wgate, wout, side, xmask, omask, xrows, kept, gain):
    vmem = pl.BlockSpec(memory_space=pltpu.VMEM)
    smem = pl.BlockSpec(memory_space=pltpu.SMEM)
    dma = pltpu.SemaphoreType.DMA
    return pl.pallas_call(
        layer_kernel,
        out_shape=(
            jax.ShapeDtypeStruct((ROWS, WIDTH), BF16),
            jax.ShapeDtypeStruct((SLOTS, WIDTH, NSTATE), F32),
        ),
        in_specs=[smem] * 4 + [vmem] * 9,
        out_specs=(vmem, vmem),
        scratch_shapes=[
            pltpu.VMEM((WIDTH, WIDE), BF16),
            pltpu.VMEM((WIDTH, WIDTH), BF16),
            pltpu.VMEM((16, WIDTH, WIDE), BF16),
            pltpu.VMEM((16, WIDTH, WIDTH), BF16),
            pltpu.VMEM((2, 512, WIDE), BF16),
            pltpu.VMEM((8, ROWS, 256), BF16),
            pltpu.VMEM((8, 288, 128), BF16),
            pltpu.VMEM((2, ROWS, 256), BF16),
            pltpu.VMEM((SLOTS, WIDTH, NSTATE), BF16),
            pltpu.VMEM((8, 128), jnp.int32),
            pltpu.VMEM((SLOTS, WIDTH, NSTATE), BF16),
            pltpu.VMEM((4, 8, 128), jnp.int32),
            pltpu.SMEM((4, 8, 128), jnp.int32),
            pltpu.SMEM((SLOTS,), jnp.int32),
            pltpu.VMEM((ROWS, WIDE), F32),
            pltpu.VMEM((3, ROWS, 256), BF16),
            pltpu.VMEM((3, ROWS, 256), BF16),
            pltpu.VMEM((MIXES, 640), BF16),
            pltpu.VMEM((8, MIXES, 640), BF16),
            pltpu.VMEM((640, 128), F32),
            pltpu.VMEM((640, NSTATE), BF16),
            pltpu.VMEM((640, NSTATE), BF16),
            pltpu.VMEM((ROWS, 128), F32),
            pltpu.VMEM((2, ROWS, WIDTH), BF16),
        ]
        + [pltpu.VMEM((4, ROWS, WIDTH), BF16)] * 4
        + [dma((2, 4))] * 8
        + [dma((2, 16))] * 2
        + [dma((4, 3))] * 4
        + [dma((4,))] * 4
        + [dma((3, 2))] * 2
        + [dma((7,))] * 2
        + [dma((4,))] * 2
        + [dma((4, 4))] * 4
        + [dma],
        compiler_params=pltpu.CompilerParams(
            collective_id=0, has_side_effects=True, vmem_limit_bytes=58 * 1024 * 1024
        ),
        name="layer",
    )(moved, bias, rate, skip, wx, wgate, wout, side, xmask, omask, xrows, kept, gain)


def on_device(
    frames_in,
    kept_state,
    moved_to,
    xz_weight,
    side_weight,
    xz_mask,
    dt_bias,
    decay_rate,
    skip_gain,
    norm_gain,
    out_weight,
    out_mask,
):
    mixed, carry = layer(
        moved_to,
        dt_bias,
        decay_rate,
        skip_gain,
        xz_weight[:, 0, :],
        xz_weight[:, 1, :],
        out_weight,
        side_weight,
        xz_mask.transpose(1, 0, 2),
        out_mask,
        frames_in.reshape(ROWS, WIDTH),
        kept_state.reshape(SLOTS, WIDTH, NSTATE),
        norm_gain.reshape(1, WIDTH),
    )
    return (
        mixed.reshape(SLOTS, FRAMES, TOKENS // FRAMES, WIDTH),
        carry.reshape(SLOTS, 5, 64, NSTATE),
    )


def solution(mesh):
    placed = (
        P("stream", None, None, "shard"),
        P("stream", "shard", None, None),
        P("stream"),
        P("stream", None, "shard"),
        P("stream", None),
        P(),
        P("shard"),
        P("shard"),
        P("shard"),
        P("shard"),
        P("stream", "shard"),
        P(),
    )
    return jax.shard_map(
        on_device,
        mesh=mesh,
        in_specs=placed,
        out_specs=(P("stream", None, None, "shard"), P("stream", "shard", None, None)),
        check_vma=False,
    )
```

```python
import jax
import jax.numpy as jnp
from jax import lax
from jax.experimental import pallas as pl
from jax.experimental.pallas import tpu as pltpu
from jax.sharding import PartitionSpec as P

MESH = pl.DeviceIdType.MESH
F32, BF16 = jnp.float32, jnp.bfloat16

NSTATE = 128
BLOCK = 128
FRAMES = 4
MOST = 3
HOPS = (1, 2, 3, 8)
ROWS = 576
SLOTS = 12
TOKENS = 48
WIDTH = 320
WIDE = 640
COLUMNS = (slice(0, 256), slice(256, 512), slice(512, 640))
MIXES = 32
SIDE = 64
SIDE_AT = 32
QUARTER = 144
NT, NN, TN = ((1,), (1,)), ((1,), (0,)), ((0,), (0,))


def place():
    si, ki = lax.axis_index("stream"), lax.axis_index("shard")
    return si // 4, (si // 2) % 2, si % 2, ki // 2, ki % 2


def device(x, y, c, z):
    return {"stream": 4 * x + 2 * (y // 2) + c, "shard": 2 * z + y % 2}


def remote(src, dst, send, recv, where):
    return pltpu.make_async_remote_copy(
        src_ref=src, dst_ref=dst, send_sem=send, recv_sem=recv, device_id=where, device_id_type=MESH
    )


def dot(a, b, dims):
    return lax.dot_general(a, b, (dims, ((), ())), preferred_element_type=F32)


def iota(shape, axis):
    return lax.broadcasted_iota(jnp.int32, shape, axis)


def halves(value):
    high = value.astype(BF16)
    return high, (value - high.astype(F32)).astype(BF16)


def layer_kernel(
    moved_ref, bias_ref, rate_ref, skip_ref,
    wx_ref, wgate_ref, wout_ref, side_ref, xmask_ref, omask_ref, x_ref, kept_ref, gain_ref,
    mixed_ref, carry_ref,
    w1, w2, ws, wg, wo, wsg, wrem, wsr, xm, xr, xk, st, sl, got, gsl, gsl_s, perm,
    xz, psend, precv, ssend, srecv, bct, bc, tile, mix_in, mix_out, steps,
    both, sendp, recvp, sendm, recvm,
    ysend, yrecv, xps, xpr, xms, xmr, x2s, x2r, ss, sr,
    zps, zpr, zms, zmr, sts, strv, sls, slr, psn, prc, bcs, bcr,
    ns, nr, ps, pr, ms, mr, local, sps, spr,
):
    x, yh, c, z, yl = place()
    y = 2 * yh + yl
    si, ki = lax.axis_index("stream"), lax.axis_index("shard")
    here = 4 * x + y
    xrt, xlt = (x + 1) % 4, (x + 3) % 4
    up = {"stream": si, "shard": 2 * ((z + 1) % 8) + yl}
    down = {"stream": si, "shard": 2 * ((z + 7) % 8) + yl}
    partner = {"stream": si, "shard": 2 * z + 1 - yl}
    peer = device(x, y, 1 - c, z)

    barrier = pltpu.get_barrier_semaphore()

    @pl.loop(1, 32)
    def _(i):
        other = (si * 2 + yl + i) % 32
        pl.semaphore_signal(
            barrier, inc=1, device_id={"stream": other // 2, "shard": 2 * z + other % 2}, device_id_type=MESH
        )

    @pl.loop(1, 8)
    def _(i):
        pl.semaphore_signal(
            barrier, inc=1, device_id={"stream": si, "shard": 2 * ((z + i) % 8) + yl}, device_id_type=MESH
        )

    xm[z] = x_ref[:, 0:256]
    xr[z] = jnp.concatenate([x_ref[0:288, 256:320], x_ref[288:576, 256:320]], axis=1)

    rows_of = (iota((WIDTH, 40), 1) == (si * WIDTH + iota((WIDTH, 40), 0)) // BLOCK).astype(BF16)
    cols_of = (iota((40, WIDTH), 0) == (ki * WIDTH + iota((40, WIDTH), 1)) // BLOCK).astype(BF16)

    def keep(mask):
        return dot(dot(rows_of, mask.astype(F32).astype(BF16), NN).astype(BF16), cols_of, NN).astype(BF16)

    pick, pick_row = iota((SIDE, 336), 0), iota((SIDE, 336), 1)
    chosen = jnp.where(pick < MIXES, pick + MIXES * z, pick - MIXES + 2 * NSTATE + 5 * ki)
    chosen = (pick_row == chosen) & (pick < MIXES + 5)
    ws[...] = dot(chosen.astype(F32).astype(BF16), side_ref[...], NT).astype(BF16)
    inner, gates = wx_ref[...] * keep(xmask_ref[0]), wgate_ref[...] * keep(xmask_ref[1])
    w1[:, 0:256] = inner[:, 0:256]
    w1[:, 256:512] = gates[:, 0:256]
    w1[:, 512:640] = jnp.concatenate([inner[:, 256:320], gates[:, 256:320]], axis=1)

    pl.semaphore_wait(barrier, 38)

    pairs = ((w1, wg), (w2, wo), (ws, wsg))
    sizes = (WIDTH // 2, WIDTH // 2, SIDE // 2)

    def half(w, core):
        return pl.ds(pl.multiple_of(core * sizes[w], sizes[w]), sizes[w])

    def y_copies(w):
        own, full = pairs[w]
        for a in range(2):
            for h in range(2):
                part = pl.ds(h * sizes[w], sizes[w])
                to = c + 2 * a
                mine = (to == y) & (c == h)
                yield mine, remote(
                    own.at[part], full.at[here, part], ysend.at[w, 2 * a + h], yrecv.at[w, y], device(x, to, h, z)
                ), pltpu.make_async_copy(own.at[part], full.at[here, part], yrecv.at[w, y])

    def y_start(w):
        for mine, far, near in y_copies(w):
            @pl.when(mine)
            def _():
                near.start()

            @pl.when(jnp.logical_not(mine))
            def _():
                far.start()

    def y_finish(w):
        for mine, far, near in y_copies(w):
            @pl.when(jnp.logical_not(mine))
            def _():
                far.wait_send()

    def block(w, x_of, ys, core=c):
        return pairs[w][1].at[4 * x_of + ys, half(w, core)]

    def hop(w, x_of, ys, send, recv, x_to):
        ref = block(w, x_of, ys)
        return remote(ref, ref, send.at[w, ys], recv.at[w, ys], device(x_to, y, c, z))

    def sibling(w, q, x_of, ys):
        ref = block(w, x_of, ys)
        return remote(ref, ref, ss.at[w, 4 * q + ys], sr.at[w, 4 * q + ys], peer)

    def landed(w, x_of, ys, recv):
        ref = block(w, x_of, ys)
        remote(ref, ref, recv.at[w, ys], recv.at[w, ys], peer).wait_recv()

    def stage_x(w, ys):
        landed(w, x, ys, yrecv)
        hop(w, x, ys, xps, xpr, xrt).start()
        hop(w, x, ys, xms, xmr, xlt).start()
        sibling(w, 0, x, ys).start()

    def stage_far(w, ys):
        landed(w, xlt, ys, xpr)
        if ys < 2:
            hop(w, xlt, ys, x2s, x2r, xrt).start()
        sibling(w, 1, xlt, ys).start()
        landed(w, xrt, ys, xmr)
        if ys >= 2:
            hop(w, xrt, ys, x2s, x2r, xlt).start()
        sibling(w, 2, xrt, ys).start()

    def stage_last(w, ys):
        landed(w, (x + 2) % 4, ys, x2r)
        sibling(w, 3, (x + 2) % 4, ys).start()

    def finish(w):
        y_finish(w)
        for q, x_of in enumerate((x, xlt, xrt, (x + 2) % 4)):
            for ys in range(4):
                sibling(w, q, x_of, ys).wait_send()
                ref = block(w, x_of, ys, 1 - c)
                remote(ref, ref, sr.at[w, 4 * q + ys], sr.at[w, 4 * q + ys], peer).wait_recv()
        for ys in range(4):
            hop(w, x, ys, xps, xpr, xrt).wait_send()
            hop(w, x, ys, xms, xmr, xlt).wait_send()
            hop(w, xlt if ys < 2 else xrt, ys, x2s, x2r, xrt if ys < 2 else xlt).wait_send()

    def piece(t, sign, g, src):
        if g == 2:
            part = pl.ds(0, 288) if t < 3 else pl.ds(0 if sign > 0 else 144, 144)
            return xr.at[src, part]
        if t < 3:
            return xm.at[src, pl.ds(288 * g, 288)]
        return xm.at[src, pl.ds((0 if sign > 0 else 288) + 144 * g, 144)]

    def ring(t, sign, g):
        ref = piece(t, sign, g, (z - sign * t + 8) % 8)
        if sign > 0:
            return remote(ref, ref, zps.at[t, g], zpr.at[t, g], up)
        return remote(ref, ref, zms.at[t, g], zmr.at[t, g], down)

    def ring_start(t):
        for g in range(3):
            for sign in (1, -1):
                if 0 < t < 3:
                    ring_land(t - 1, sign, g)
                ring(t, sign, g).start()

    def ring_land(t, sign, g):
        ref = piece(t, sign, g, (z - sign * (t + 1) + 8) % 8)
        sem = zpr if sign > 0 else zmr
        remote(ref, ref, sem.at[t, g], sem.at[t, g], up).wait_recv()

    def states():
        for t, hops in enumerate(HOPS):
            where = {"stream": (si + hops) % 16, "shard": ki}
            yield remote(st.at[pl.ds(MOST * t, MOST)], got.at[pl.ds(MOST * t, MOST)], sts.at[t], strv.at[t], where)
            yield remote(sl, gsl.at[t], sls.at[t], slr.at[t], where)

    y_start(2)
    y_start(0)
    ring_start(0)
    w2[...] = wout_ref[...] * keep(omask_ref[...])
    y_start(1)
    for ys in range(4):
        stage_x(2, ys)
    stage_x(0, 0)
    stage_x(0, 1)

    ways = [jnp.minimum((moved_ref[j] // SLOTS - si + 16) % 16 - 1, 3) for j in range(SLOTS)]
    spots = []
    for j in range(SLOTS):
        rank = sum(((ways[i] == ways[j]).astype(jnp.int32) for i in range(j)), jnp.int32(0))
        spots.append(MOST * ways[j] + rank)
    lane = iota((8, 128), 1)
    slots = jnp.zeros((8, 128), jnp.int32)
    for j in range(SLOTS):
        slots = jnp.where(lane == spots[j], moved_ref[j] % SLOTS, slots)
    sl[...] = slots
    stage_x(0, 2)
    stage_x(0, 3)
    for p in range(SLOTS):
        source = sum((jnp.where(spots[j] == p, j, 0) for j in range(1, SLOTS)), jnp.int32(0))
        st[p] = kept_ref[jnp.minimum(source, SLOTS - 1)].astype(BF16)
    ring_start(1)
    for ys in range(4):
        stage_far(2, ys)
    stage_far(0, 0)
    stage_far(0, 1)
    ring_start(2)
    for ys in range(4):
        stage_last(2, ys)
    stage_far(0, 2)
    stage_far(0, 3)
    for copy in states():
        copy.start()
    for g in range(3):
        for sign in (1, -1):
            ring_land(2, sign, g)
    ring_start(3)
    finish(2)
    stage_last(0, 0)
    stage_last(0, 1)
    for g in range(3):
        for sign in (1, -1):
            ring_land(3, sign, g)

    low = iota((288, 128), 1) < 64
    for i in range(4):
        first, second = xr[2 * i].astype(F32), xr[2 * i + 1].astype(F32)
        lanes = slice(128 * (i % 2), 128 * (i % 2) + 128)
        xk[i // 2, 0:288, lanes] = jnp.where(low, first, pltpu.roll(second, 64, 1)).astype(BF16)
        xk[i // 2, 288:576, lanes] = jnp.where(low, pltpu.roll(first, 64, 1), second).astype(BF16)
    for j in range(8):
        for b in range(2):
            lanes = slice(64 * (j % 4), 64 * (j % 4) + 64)
            wsr[b, j // 4, :, lanes] = wsg[4 * (j // 2) + 2 * (j % 2) + b, :, 256:320]

    def side_sums(b):
        total = None
        for j in range(8):
            one = dot(wsg[4 * (j // 2) + 2 * (j % 2) + b, :, 0:256], xm[j], NT)
            total = one if total is None else total + one
        for i in range(2):
            total = total + dot(wsr[b, i], xk[i], NT)
        return total

    def mixes(i):
        return remote(bct, bc.at[z], bcs.at[i], bcr.at[i], {"stream": si, "shard": 2 * ((z + i + 1) % 8) + yl})

    ssend[...] = side_sums(1 - yl).astype(BF16)
    side_swap = remote(ssend, srecv, sps, spr, partner)
    side_swap.start()
    tile[...] = jnp.zeros_like(tile)
    tile[0:SIDE, 0:ROWS] = side_sums(yl)
    stage_last(0, 2)
    stage_last(0, 3)
    side_swap.wait()
    tile[0:SIDE, 0:ROWS] += srecv[...].astype(F32)
    bct[...] = tile[0:MIXES, :].astype(BF16)
    bc[z] = bct[...]
    for i in range(7):
        mixes(i).start()

    finish(0)
    for j in range(8):
        for b in range(2):
            wrem[b, 64 * j : 64 * j + 64, :] = wg[4 * (j // 2) + 2 * (j % 2) + b, 256:320, :]

    def matmul(b, n, r):
        rows = slice(288 * r, 288 * r + 288)
        total = None
        for j in range(8):
            one = dot(xm[j, rows, :], wg[4 * (j // 2) + 2 * (j % 2) + b, 0:256, COLUMNS[n]], NN)
            total = one if total is None else total + one
        for i in range(2):
            total = total + dot(xk[i, rows, :], wrem[b, 256 * i : 256 * i + 256, COLUMNS[n]], NN)
        return total

    def rows_at(q):
        return pl.ds(QUARTER * q, QUARTER)

    def swap(q):
        return remote(psend.at[rows_at(q)], precv.at[rows_at(q)], psn.at[q], prc.at[q], partner)

    for r in range(2):
        for n in range(3):
            psend[288 * r : 288 * r + 288, COLUMNS[n]] = matmul(1 - yl, n, r).astype(BF16)
        swap(2 * r).start()
        swap(2 * r + 1).start()
    for ys in range(4):
        stage_x(1, ys)
    for r in range(2):
        for n in range(3):
            xz[288 * r : 288 * r + 288, COLUMNS[n]] = matmul(yl, n, r)

    for copy in states():
        copy.wait()
    fetch = pltpu.make_async_copy(gsl, gsl_s, local)
    fetch.start()
    raw_bias = jnp.zeros((1, 128), F32)
    rate = jnp.zeros((1, 128), F32)
    skip = jnp.zeros((1, WIDTH), F32)
    for h in range(5):
        raw_bias = jnp.where(iota((1, 128), 1) == SIDE_AT + h, bias_ref[h], raw_bias)
        rate = jnp.where(iota((1, 128), 1) == SIDE_AT + h, rate_ref[h], rate)
        skip = jnp.where(iota((1, WIDTH), 1) // 64 == h, skip_ref[h], skip)
    gain = gain_ref[...]
    raw = tile[...].T + raw_bias
    live = (iota((1, 128), 1) >= SIDE_AT) & (iota((1, 128), 1) < SIDE_AT + 5)
    steps[...] = jnp.where(live, jnp.maximum(raw, 0.0) + jnp.log1p(jnp.exp(-jnp.abs(raw))), 0.0)
    fetch.wait()
    landing = [gsl_s[j // MOST, 0, j] for j in range(SLOTS)]
    for s in range(SLOTS):
        found = sum((jnp.where(landing[j] == s, j, 0) for j in range(1, SLOTS)), jnp.int32(0))
        perm[s] = jnp.minimum(found, SLOTS - 1)

    for i in range(7):
        src = (z + 7 - i) % 8
        remote(bct, bc.at[src], bcr.at[i], bcr.at[i], partner).wait_recv()
    mix_in[...] = bc[0:4].reshape(NSTATE, 640).astype(F32).T.astype(BF16)
    mix_out[...] = bc[4:8].reshape(NSTATE, 640).astype(F32).T.astype(BF16)

    spread = jnp.concatenate(
        [
            iota((128, 384), 0) == SIDE_AT + iota((128, 384), 1) // 64,
            (iota((128, 256), 0) == SIDE_AT + iota((128, 256), 1) // TOKENS) & (iota((128, 256), 1) < 240),
        ],
        axis=1,
    ).astype(F32).astype(BF16)
    spread = jnp.concatenate([spread, spread], axis=0)
    in_order = iota((TOKENS, TOKENS), 0) >= iota((TOKENS, TOKENS), 1)
    lower = in_order.astype(F32).astype(BF16)
    token_of = iota((TOKENS, 240), 1) % TOKENS
    causal = iota((TOKENS, 240), 0) >= token_of
    same = iota((TOKENS, 240), 0) == token_of
    head_of = iota((TOKENS, WIDTH), 1) // 64
    ones = jnp.ones((16, NSTATE), BF16)

    def scan(q):
        swap(q).wait_recv()
        xz[rows_at(q), :] += precv[rows_at(q), :].astype(F32)

        @pl.loop(0, 3)
        def _(i):
            s = 3 * q + i
            rows = pl.ds(pl.multiple_of(s * TOKENS, TOKENS), TOKENS)
            step = steps[rows, :]
            step_parts = halves(step)
            decay_parts = halves(-rate * step)
            cumulative = dot(lower, decay_parts[0], NN) + dot(lower, decay_parts[1], NN)
            cum_all = dot(jnp.concatenate(halves(cumulative), axis=1), spread, NN)
            step_wide = dot(jnp.concatenate(step_parts, axis=1), spread[:, 0:384], NN)[:, 0:WIDTH]
            cum_wide = cum_all[:, 0:WIDTH]
            cum_left = cum_all[:, 384:624]
            cum_right = jnp.sum(jnp.where(same, cum_left, 0.0), axis=0, keepdims=True)
            b_s, c_s = mix_in[rows, :], mix_out[rows, :]
            scores = dot(c_s, jnp.concatenate([b_s] * 5, axis=0), NT)
            mixing = jnp.where(causal, jnp.exp(jnp.where(causal, cum_left - cum_right, 0.0)) * scores, 0.0).astype(BF16)
            inputs = jnp.concatenate([xz[rows, 0:256], xz[rows, 512:576]], axis=1)
            stepped = inputs * step_wide
            stepped_b = stepped.astype(BF16)
            blocks = jnp.concatenate(
                [jnp.where(head_of == h, stepped_b, jnp.zeros_like(stepped_b)) for h in range(5)], axis=0
            )
            state = got[perm[s]]
            out = dot(mixing, blocks, NN)
            out += jnp.exp(cum_wide) * dot(c_s, state, NT)
            out += skip * inputs
            last = cum_wide[TOKENS - 1 : TOKENS, :]
            to_end = (jnp.exp(last - cum_wide) * stepped).astype(BF16)
            fade_high, fade_low = halves(jnp.exp(last))
            first = iota((16, WIDTH), 0)
            zero = jnp.zeros((16, WIDTH), BF16)
            fade = jnp.where(first == 0, fade_high, jnp.where(first == 1, fade_low, zero))
            carry_ref[s] = dot(fade, ones, TN) * state.astype(F32) + dot(to_end, b_s, TN)
            gate = jnp.concatenate([xz[rows, 256:512], xz[rows, 576:640]], axis=1)
            gated = out * gate * (1.0 / (1.0 + jnp.exp(-gate)))
            mean_square = jnp.sum(gated * gated, axis=1, keepdims=True) * (1.0 / WIDTH)
            both[yl, rows, :] = (gated * lax.rsqrt(mean_square + 1e-05) * gain).astype(BF16)

    def give(q):
        ref = both.at[yl, rows_at(q)]
        return remote(ref, ref, ns.at[q], nr.at[q], partner)

    def given(q):
        ref = both.at[1 - yl, rows_at(q)]
        remote(ref, ref, nr.at[q], nr.at[q], partner).wait_recv()

    def term(to, q):
        at = 4 * (to // 2) + 2 * (to % 2)
        return dot(both[0, rows_at(q), :], wo[at], NT) + dot(both[1, rows_at(q), :], wo[at + 1], NT)

    def relay(sign, t, q):
        if sign > 0:
            return remote(sendp.at[t, rows_at(q)], recvp.at[t, rows_at(q)], ps.at[t, q], pr.at[t, q], up)
        return remote(sendm.at[t, rows_at(q)], recvm.at[t, rows_at(q)], ms.at[t, q], mr.at[t, q], down)

    def starts(sign, q):
        return 0 if (q < 2) == (sign > 0) else 1

    def go(t, q):
        for sign in (1, -1):
            if t < starts(sign, q):
                continue
            value = term((z + 8 + sign * (4 - t)) % 8, q)
            send, recv = (sendp, recvp) if sign > 0 else (sendm, recvm)
            if t > starts(sign, q):
                relay(sign, t - 1, q).wait_recv()
                value = value + recv[t - 1, rows_at(q), :].astype(F32)
            send[t, rows_at(q), :] = value.astype(BF16)
            relay(sign, t, q).start()

    def arrive(q):
        value = term(z, q)
        relay(1, 3, q).wait_recv()
        relay(-1, 3, q).wait_recv()
        value = value + recvp[3, rows_at(q), :].astype(F32) + recvm[3, rows_at(q), :].astype(F32)
        mixed_ref[rows_at(q), :] = value.astype(BF16)

    scan(0)
    give(0).start()
    for ys in range(4):
        stage_far(1, ys)
    scan(1)
    give(1).start()
    for ys in range(4):
        stage_last(1, ys)
    finish(1)
    given(0)
    go(0, 0)
    scan(2)
    give(2).start()
    given(1)
    go(0, 1)
    go(1, 0)
    scan(3)
    give(3).start()
    go(1, 1)
    given(2)
    go(0, 2)
    go(2, 0)
    given(3)
    go(0, 3)
    go(1, 2)
    go(2, 1)
    go(3, 0)
    go(1, 3)
    go(2, 2)
    go(3, 1)
    go(2, 3)
    arrive(0)
    go(3, 2)
    arrive(1)
    go(3, 3)
    arrive(2)
    arrive(3)

    for q in range(4):
        give(q).wait_send()
        for sign in (1, -1):
            for t in range(starts(sign, q), 4):
                relay(sign, t, q).wait_send()
        swap(q).wait_send()
    for i in range(7):
        mixes(i).wait_send()
    for t in range(4):
        for g in range(3):
            ring(t, 1, g).wait_send()
            ring(t, -1, g).wait_send()


def layer(moved, bias, rate, skip, wx, wgate, wout, side, xmask, omask, xrows, kept, gain):
    vmem = pl.BlockSpec(memory_space=pltpu.VMEM)
    smem = pl.BlockSpec(memory_space=pltpu.SMEM)
    dma = pltpu.SemaphoreType.DMA
    return pl.pallas_call(
        layer_kernel,
        out_shape=(
            jax.ShapeDtypeStruct((ROWS, WIDTH), BF16),
            jax.ShapeDtypeStruct((SLOTS, WIDTH, NSTATE), F32),
        ),
        in_specs=[smem] * 4 + [vmem] * 9,
        out_specs=(vmem, vmem),
        scratch_shapes=[
            pltpu.VMEM((WIDTH, WIDE), BF16),
            pltpu.VMEM((WIDTH, WIDTH), BF16),
            pltpu.VMEM((SIDE, WIDTH), BF16),
            pltpu.VMEM((16, WIDTH, WIDE), BF16),
            pltpu.VMEM((16, WIDTH, WIDTH), BF16),
            pltpu.VMEM((16, SIDE, WIDTH), BF16),
            pltpu.VMEM((2, 512, WIDE), BF16),
            pltpu.VMEM((2, 2, SIDE, 256), BF16),
            pltpu.VMEM((8, ROWS, 256), BF16),
            pltpu.VMEM((8, 288, 128), BF16),
            pltpu.VMEM((2, ROWS, 256), BF16),
            pltpu.VMEM((SLOTS, WIDTH, NSTATE), BF16),
            pltpu.VMEM((8, 128), jnp.int32),
            pltpu.VMEM((SLOTS, WIDTH, NSTATE), BF16),
            pltpu.VMEM((4, 8, 128), jnp.int32),
            pltpu.SMEM((4, 8, 128), jnp.int32),
            pltpu.SMEM((SLOTS,), jnp.int32),
            pltpu.VMEM((ROWS, WIDE), F32),
            pltpu.VMEM((ROWS, WIDE), BF16),
            pltpu.VMEM((ROWS, WIDE), BF16),
            pltpu.VMEM((SIDE, ROWS), BF16),
            pltpu.VMEM((SIDE, ROWS), BF16),
            pltpu.VMEM((MIXES, 640), BF16),
            pltpu.VMEM((8, MIXES, 640), BF16),
            pltpu.VMEM((128, 640), F32),
            pltpu.VMEM((640, NSTATE), BF16),
            pltpu.VMEM((640, NSTATE), BF16),
            pltpu.VMEM((640, 128), F32),
            pltpu.VMEM((2, ROWS, WIDTH), BF16),
        ]
        + [pltpu.VMEM((4, ROWS, WIDTH), BF16)] * 4
        + [dma((3, 4))] * 8
        + [dma((3, 16))] * 2
        + [dma((4, 3))] * 4
        + [dma((4,))] * 4
        + [dma((4,))] * 2
        + [dma((7,))] * 2
        + [dma((4,))] * 2
        + [dma((4, 4))] * 4
        + [dma] * 3,
        compiler_params=pltpu.CompilerParams(
            collective_id=0, has_side_effects=True, vmem_limit_bytes=58 * 1024 * 1024
        ),
        name="layer",
    )(moved, bias, rate, skip, wx, wgate, wout, side, xmask, omask, xrows, kept, gain)


def on_device(
    frames_in,
    kept_state,
    moved_to,
    xz_weight,
    side_weight,
    xz_mask,
    dt_bias,
    decay_rate,
    skip_gain,
    norm_gain,
    out_weight,
    out_mask,
):
    mixed, carry = layer(
        moved_to,
        dt_bias,
        decay_rate,
        skip_gain,
        xz_weight[:, 0, :],
        xz_weight[:, 1, :],
        out_weight,
        side_weight,
        xz_mask.transpose(1, 0, 2),
        out_mask,
        frames_in.reshape(ROWS, WIDTH),
        kept_state.reshape(SLOTS, WIDTH, NSTATE),
        norm_gain.reshape(1, WIDTH),
    )
    return (
        mixed.reshape(SLOTS, FRAMES, TOKENS // FRAMES, WIDTH),
        carry.reshape(SLOTS, 5, 64, NSTATE),
    )


def solution(mesh):
    placed = (
        P("stream", None, None, "shard"),
        P("stream", "shard", None, None),
        P("stream"),
        P("stream", None, "shard"),
        P("stream", None),
        P(),
        P("shard"),
        P("shard"),
        P("shard"),
        P("shard"),
        P("stream", "shard"),
        P(),
    )
    return jax.shard_map(
        on_device,
        mesh=mesh,
        in_specs=placed,
        out_specs=(P("stream", None, None, "shard"), P("stream", "shard", None, None)),
        check_vma=False,
    )
```

```python
import jax
import jax.numpy as jnp
from jax import lax
from jax.experimental import pallas as pl
from jax.experimental.pallas import tpu as pltpu
from jax.sharding import PartitionSpec as P

MESH = pl.DeviceIdType.MESH
F32, BF16 = jnp.float32, jnp.bfloat16

NSTATE = 128
BLOCK = 128
FRAMES = 4
MOST = 3
HOPS = (1, 2, 3, 8)
ROWS = 576
SLOTS = 12
TOKENS = 48
WIDTH = 320
WIDE = 640
COLUMNS = (slice(0, 256), slice(256, 512), slice(512, 640))
MIXES = 32
SIDE = 64
SIDE_AT = 32
PACKED = 416
QUARTER = 144
NT, NN, TN = ((1,), (1,)), ((1,), (0,)), ((0,), (0,))


def place():
    si, ki = lax.axis_index("stream"), lax.axis_index("shard")
    return si // 4, (si // 2) % 2, si % 2, ki // 2, ki % 2


def device(x, y, c, z):
    return {"stream": 4 * x + 2 * (y // 2) + c, "shard": 2 * z + y % 2}


def remote(src, dst, send, recv, where):
    return pltpu.make_async_remote_copy(
        src_ref=src, dst_ref=dst, send_sem=send, recv_sem=recv, device_id=where, device_id_type=MESH
    )


def dot(a, b, dims):
    return lax.dot_general(a, b, (dims, ((), ())), preferred_element_type=F32)


def iota(shape, axis):
    return lax.broadcasted_iota(jnp.int32, shape, axis)


def halves(value):
    high = value.astype(BF16)
    return high, (value - high.astype(F32)).astype(BF16)


def layer_kernel(
    moved_ref, bias_ref, rate_ref, skip_ref,
    win_ref, wout_ref, side_ref, xmask_ref, omask_ref, x_ref, kept_ref, gain_ref,
    mixed_ref, carry_ref,
    w1, w2, ws, wg, wo, worem, wsg, wrem, wsr, xm, xr, xk, st, sl, st8, sl8, got, gsl, gsl_s, perm,
    xz, psend, precv, ssend, srecv, bct, bc, tile, mix_in, mix_out, steps,
    both, bothr, sendp, recvp, sendm, recvm,
    ysend, yrecv, xps, xpr, xms, xmr, x2s, x2r, ss, sr,
    zps, zpr, zms, zmr, sts, strv, sls, slr, psn, prc, bcs, bcr,
    ns, nr, ps, pr, ms, mr, local, sps, spr, rls, rlr,
):
    x, yh, c, z, yl = place()
    y = 2 * yh + yl
    si, ki = lax.axis_index("stream"), lax.axis_index("shard")
    here = 4 * x + y
    xrt, xlt = (x + 1) % 4, (x + 3) % 4
    up = {"stream": si, "shard": 2 * ((z + 1) % 8) + yl}
    down = {"stream": si, "shard": 2 * ((z + 7) % 8) + yl}
    partner = {"stream": si, "shard": 2 * z + 1 - yl}
    peer = device(x, y, 1 - c, z)

    barrier = pltpu.get_barrier_semaphore()

    @pl.loop(1, 32)
    def _(i):
        other = (si * 2 + yl + i) % 32
        pl.semaphore_signal(
            barrier, inc=1, device_id={"stream": other // 2, "shard": 2 * z + other % 2}, device_id_type=MESH
        )

    @pl.loop(1, 8)
    def _(i):
        pl.semaphore_signal(
            barrier, inc=1, device_id={"stream": si, "shard": 2 * ((z + i) % 8) + yl}, device_id_type=MESH
        )

    xm[z] = x_ref[:, 0:256]
    xr[z] = jnp.concatenate([x_ref[0:288, 256:320], x_ref[288:576, 256:320]], axis=1)

    rows_of = (iota((WIDTH, 40), 1) == (si * WIDTH + iota((WIDTH, 40), 0)) // BLOCK).astype(BF16)
    cols_of = (iota((40, WIDTH), 0) == (ki * WIDTH + iota((40, WIDTH), 1)) // BLOCK).astype(BF16)

    def keep(mask):
        return dot(dot(rows_of, mask.astype(F32).astype(BF16), NN).astype(BF16), cols_of, NN).astype(BF16)

    pick, pick_row = iota((SIDE, 336), 0), iota((SIDE, 336), 1)
    chosen = jnp.where(pick < MIXES, pick + MIXES * z, pick - MIXES + 2 * NSTATE + 5 * ki)
    chosen = (pick_row == chosen) & (pick < MIXES + 5)
    ws[...] = dot(chosen.astype(F32).astype(BF16), side_ref[...], NT).astype(BF16)
    inner, gates = win_ref[:, 0, :] * keep(xmask_ref[:, 0, :]), win_ref[:, 1, :] * keep(xmask_ref[:, 1, :])
    w1[:, 0:256] = inner[:, 0:256]
    w1[:, 256:512] = gates[:, 0:256]
    w1[:, 512:640] = jnp.concatenate([inner[:, 256:320], gates[:, 256:320]], axis=1)

    pl.semaphore_wait(barrier, 38)

    pairs = ((w1, wg), (w2, wo), (ws, wsg))
    sizes = (WIDTH // 2, PACKED // 2, SIDE // 2)

    def half(w, core):
        return pl.ds(pl.multiple_of(core * sizes[w], sizes[w]), sizes[w])

    def y_copies(w):
        own, full = pairs[w]
        for a in range(2):
            for h in range(2):
                part = pl.ds(h * sizes[w], sizes[w])
                to = c + 2 * a
                mine = (to == y) & (c == h)
                yield mine, remote(
                    own.at[part], full.at[here, part], ysend.at[w, 2 * a + h], yrecv.at[w, y], device(x, to, h, z)
                ), pltpu.make_async_copy(own.at[part], full.at[here, part], yrecv.at[w, y])

    def y_start(w):
        for mine, far, near in y_copies(w):
            @pl.when(mine)
            def _():
                near.start()

            @pl.when(jnp.logical_not(mine))
            def _():
                far.start()

    def y_finish(w):
        for mine, far, near in y_copies(w):
            @pl.when(jnp.logical_not(mine))
            def _():
                far.wait_send()

    def block(w, x_of, ys, core=c):
        return pairs[w][1].at[4 * x_of + ys, half(w, core)]

    def hop(w, x_of, ys, send, recv, x_to):
        ref = block(w, x_of, ys)
        return remote(ref, ref, send.at[w, ys], recv.at[w, ys], device(x_to, y, c, z))

    def sibling(w, q, x_of, ys):
        ref = block(w, x_of, ys)
        return remote(ref, ref, ss.at[w, 4 * q + ys], sr.at[w, 4 * q + ys], peer)

    def landed(w, x_of, ys, recv):
        ref = block(w, x_of, ys)
        remote(ref, ref, recv.at[w, ys], recv.at[w, ys], peer).wait_recv()

    def stage_x(w, ys):
        landed(w, x, ys, yrecv)
        hop(w, x, ys, xps, xpr, xrt).start()
        hop(w, x, ys, xms, xmr, xlt).start()
        sibling(w, 0, x, ys).start()

    def stage_far(w, ys):
        landed(w, xlt, ys, xpr)
        if ys < 2:
            hop(w, xlt, ys, x2s, x2r, xrt).start()
        sibling(w, 1, xlt, ys).start()
        landed(w, xrt, ys, xmr)
        if ys >= 2:
            hop(w, xrt, ys, x2s, x2r, xlt).start()
        sibling(w, 2, xrt, ys).start()

    def stage_last(w, ys):
        landed(w, (x + 2) % 4, ys, x2r)
        sibling(w, 3, (x + 2) % 4, ys).start()

    def finish(w):
        y_finish(w)
        for q, x_of in enumerate((x, xlt, xrt, (x + 2) % 4)):
            for ys in range(4):
                sibling(w, q, x_of, ys).wait_send()
                ref = block(w, x_of, ys, 1 - c)
                remote(ref, ref, sr.at[w, 4 * q + ys], sr.at[w, 4 * q + ys], peer).wait_recv()
        for ys in range(4):
            hop(w, x, ys, xps, xpr, xrt).wait_send()
            hop(w, x, ys, xms, xmr, xlt).wait_send()
            hop(w, xlt if ys < 2 else xrt, ys, x2s, x2r, xrt if ys < 2 else xlt).wait_send()

    def piece(t, sign, g, src):
        if g == 2:
            part = pl.ds(0, 288) if t < 3 else pl.ds(0 if sign > 0 else 144, 144)
            return xr.at[src, part]
        if t < 3:
            return xm.at[src, pl.ds(288 * g, 288)]
        return xm.at[src, pl.ds((0 if sign > 0 else 288) + 144 * g, 144)]

    def ring(t, sign, g):
        ref = piece(t, sign, g, (z - sign * t + 8) % 8)
        if sign > 0:
            return remote(ref, ref, zps.at[t, g], zpr.at[t, g], up)
        return remote(ref, ref, zms.at[t, g], zmr.at[t, g], down)

    def ring_start(t):
        for g in range(3):
            for sign in (1, -1):
                if 0 < t < 3:
                    ring_land(t - 1, sign, g)
                ring(t, sign, g).start()

    def ring_land(t, sign, g):
        ref = piece(t, sign, g, (z - sign * (t + 1) + 8) % 8)
        sem = zpr if sign > 0 else zmr
        remote(ref, ref, sem.at[t, g], sem.at[t, g], up).wait_recv()

    def states():
        for t, hops in enumerate(HOPS[:3]):
            where = {"stream": (si + hops) % 16, "shard": ki}
            yield remote(st.at[pl.ds(MOST * t, MOST)], got.at[pl.ds(MOST * t, MOST)], sts.at[t], strv.at[t], where)
            yield remote(sl, gsl.at[t], sls.at[t], slr.at[t], where)

    def relays():
        where = {"stream": (si + 12) % 16, "shard": ki}
        part = pl.ds(3 * MOST, MOST)
        first = remote(st.at[part], st8, rls.at[0], rlr.at[0], where), remote(sl, sl8, rls.at[1], rlr.at[1], where)
        last = remote(st8, got.at[part], sts.at[3], strv.at[3], where), remote(sl8, gsl.at[3], sls.at[3], slr.at[3], where)
        return first, last

    y_start(2)
    y_start(0)
    ring_start(0)
    outer = wout_ref[...] * keep(omask_ref[...])
    w2[0:WIDTH, :] = outer[:, 0:256]
    w2[WIDTH : WIDTH + 80, :] = jnp.concatenate([outer[80 * g : 80 * g + 80, 256:320] for g in range(4)], axis=1)
    w2[WIDTH + 80 : PACKED, :] = jnp.zeros((16, 256), BF16)
    y_start(1)
    for ys in range(4):
        stage_x(2, ys)
    stage_x(0, 0)
    stage_x(0, 1)

    ways = [jnp.minimum((moved_ref[j] // SLOTS - si + 16) % 16 - 1, 3) for j in range(SLOTS)]
    spots = []
    for j in range(SLOTS):
        rank = sum(((ways[i] == ways[j]).astype(jnp.int32) for i in range(j)), jnp.int32(0))
        spots.append(MOST * ways[j] + rank)
    lane = iota((8, 128), 1)
    slots = jnp.zeros((8, 128), jnp.int32)
    for j in range(SLOTS):
        slots = jnp.where(lane == spots[j], moved_ref[j] % SLOTS, slots)
    sl[...] = slots
    stage_x(0, 2)
    stage_x(0, 3)
    for p in range(SLOTS):
        source = sum((jnp.where(spots[j] == p, j, 0) for j in range(1, SLOTS)), jnp.int32(0))
        st[p] = kept_ref[jnp.minimum(source, SLOTS - 1)].astype(BF16)
    ring_start(1)
    for ys in range(4):
        stage_far(2, ys)
    stage_far(0, 0)
    stage_far(0, 1)
    ring_start(2)
    for ys in range(4):
        stage_last(2, ys)
    stage_far(0, 2)
    stage_far(0, 3)
    to_relay, relayed = relays()
    for copy in to_relay:
        copy.start()
    for copy in states():
        copy.start()
    for g in range(3):
        for sign in (1, -1):
            ring_land(2, sign, g)
    ring_start(3)
    finish(2)
    stage_last(0, 0)
    stage_last(0, 1)
    for g in range(3):
        for sign in (1, -1):
            ring_land(3, sign, g)

    low = iota((288, 128), 1) < 64
    for i in range(4):
        first, second = xr[2 * i].astype(F32), xr[2 * i + 1].astype(F32)
        lanes = slice(128 * (i % 2), 128 * (i % 2) + 128)
        xk[i // 2, 0:288, lanes] = jnp.where(low, first, pltpu.roll(second, 64, 1)).astype(BF16)
        xk[i // 2, 288:576, lanes] = jnp.where(low, pltpu.roll(first, 64, 1), second).astype(BF16)
    for j in range(8):
        for b in range(2):
            lanes = slice(64 * (j % 4), 64 * (j % 4) + 64)
            wsr[b, j // 4, :, lanes] = wsg[4 * (j // 2) + 2 * (j % 2) + b, :, 256:320]

    def side_sums(b):
        total = None
        for j in range(8):
            one = dot(wsg[4 * (j // 2) + 2 * (j % 2) + b, :, 0:256], xm[j], NT)
            total = one if total is None else total + one
        for i in range(2):
            total = total + dot(wsr[b, i], xk[i], NT)
        return total

    def mixes(i):
        return remote(bct, bc.at[z], bcs.at[i], bcr.at[i], {"stream": si, "shard": 2 * ((z + i + 1) % 8) + yl})

    ssend[...] = side_sums(1 - yl).astype(BF16)
    side_swap = remote(ssend, srecv, sps, spr, partner)
    side_swap.start()
    tile[...] = jnp.zeros_like(tile)
    tile[0:SIDE, 0:ROWS] = side_sums(yl)
    for copy in to_relay:
        copy.wait_recv()
    for copy in relayed:
        copy.start()
    stage_last(0, 2)
    stage_last(0, 3)
    side_swap.wait()
    tile[0:SIDE, 0:ROWS] += srecv[...].astype(F32)
    bct[...] = tile[0:MIXES, :].astype(BF16)
    bc[z] = bct[...]
    for i in range(7):
        mixes(i).start()
    for ys in range(4):
        stage_x(1, ys)

    finish(0)
    for j in range(8):
        for b in range(2):
            wrem[b, 64 * j : 64 * j + 64, :] = wg[4 * (j // 2) + 2 * (j % 2) + b, 256:320, :]

    def matmul(b, n, r):
        rows = slice(288 * r, 288 * r + 288)
        total = None
        for j in range(8):
            one = dot(xm[j, rows, :], wg[4 * (j // 2) + 2 * (j % 2) + b, 0:256, COLUMNS[n]], NN)
            total = one if total is None else total + one
        for i in range(2):
            total = total + dot(xk[i, rows, :], wrem[b, 256 * i : 256 * i + 256, COLUMNS[n]], NN)
        return total

    def rows_at(q):
        return pl.ds(QUARTER * q, QUARTER)

    def swap(q):
        return remote(psend.at[rows_at(q)], precv.at[rows_at(q)], psn.at[q], prc.at[q], partner)

    for r in range(2):
        for n in range(3):
            psend[288 * r : 288 * r + 288, COLUMNS[n]] = matmul(1 - yl, n, r).astype(BF16)
        swap(2 * r).start()
        swap(2 * r + 1).start()
    for r in range(2):
        for n in range(3):
            xz[288 * r : 288 * r + 288, COLUMNS[n]] = matmul(yl, n, r)

    for ys in range(4):
        stage_far(1, ys)

    for copy in states():
        copy.wait()
    for copy in relayed:
        copy.wait()
    for copy in to_relay:
        copy.wait_send()
    fetch = pltpu.make_async_copy(gsl, gsl_s, local)
    fetch.start()
    raw_bias = jnp.zeros((1, 128), F32)
    rate = jnp.zeros((1, 128), F32)
    skip = jnp.zeros((1, WIDTH), F32)
    for h in range(5):
        raw_bias = jnp.where(iota((1, 128), 1) == SIDE_AT + h, bias_ref[h], raw_bias)
        rate = jnp.where(iota((1, 128), 1) == SIDE_AT + h, rate_ref[h], rate)
        skip = jnp.where(iota((1, WIDTH), 1) // 64 == h, skip_ref[h], skip)
    gain = gain_ref[...].reshape(1, WIDTH)
    raw = tile[...].T + raw_bias
    live = (iota((1, 128), 1) >= SIDE_AT) & (iota((1, 128), 1) < SIDE_AT + 5)
    steps[...] = jnp.where(live, jnp.maximum(raw, 0.0) + jnp.log1p(jnp.exp(-jnp.abs(raw))), 0.0)
    fetch.wait()
    landing = [gsl_s[j // MOST, 0, j] for j in range(SLOTS)]
    for s in range(SLOTS):
        found = sum((jnp.where(landing[j] == s, j, 0) for j in range(1, SLOTS)), jnp.int32(0))
        perm[s] = jnp.minimum(found, SLOTS - 1)

    for i in range(7):
        src = (z + 7 - i) % 8
        remote(bct, bc.at[src], bcr.at[i], bcr.at[i], partner).wait_recv()
    mix_in[...] = bc[0:4].reshape(NSTATE, 640).astype(F32).T.astype(BF16)
    mix_out[...] = bc[4:8].reshape(NSTATE, 640).astype(F32).T.astype(BF16)

    spread = jnp.concatenate(
        [
            iota((128, 384), 0) == SIDE_AT + iota((128, 384), 1) // 64,
            (iota((128, 256), 0) == SIDE_AT + iota((128, 256), 1) // TOKENS) & (iota((128, 256), 1) < 240),
        ],
        axis=1,
    ).astype(F32).astype(BF16)
    spread = jnp.concatenate([spread, spread], axis=0)
    def time(row):
        return (row % FRAMES) * (TOKENS // FRAMES) + row // FRAMES

    in_order = time(iota((TOKENS, TOKENS), 0)) >= time(iota((TOKENS, TOKENS), 1))
    lower = in_order.astype(F32).astype(BF16)
    token_of = iota((TOKENS, 240), 1) % TOKENS
    causal = time(iota((TOKENS, 240), 0)) >= time(token_of)
    same = iota((TOKENS, 240), 0) == token_of
    head_of = iota((TOKENS, WIDTH), 1) // 64
    ones = jnp.ones((16, NSTATE), BF16)

    def scan(q):
        swap(q).wait_recv()
        xz[rows_at(q), :] += precv[rows_at(q), :].astype(F32)

        @pl.loop(0, 3)
        def _(i):
            s = 3 * q + i
            rows = pl.ds(pl.multiple_of(s * TOKENS, TOKENS), TOKENS)
            step = steps[rows, :]
            step_parts = halves(step)
            decay_parts = halves(-rate * step)
            cumulative = dot(lower, decay_parts[0], NN) + dot(lower, decay_parts[1], NN)
            cum_all = dot(jnp.concatenate(halves(cumulative), axis=1), spread, NN)
            step_wide = dot(jnp.concatenate(step_parts, axis=1), spread[:, 0:384], NN)[:, 0:WIDTH]
            cum_wide = cum_all[:, 0:WIDTH]
            cum_left = cum_all[:, 384:624]
            cum_right = jnp.sum(jnp.where(same, cum_left, 0.0), axis=0, keepdims=True)
            b_s, c_s = mix_in[rows, :], mix_out[rows, :]
            scores = dot(c_s, jnp.concatenate([b_s] * 5, axis=0), NT)
            mixing = jnp.where(causal, jnp.exp(jnp.where(causal, cum_left - cum_right, 0.0)) * scores, 0.0).astype(BF16)
            inputs = jnp.concatenate([xz[rows, 0:256], xz[rows, 512:576]], axis=1)
            stepped = inputs * step_wide
            stepped_b = stepped.astype(BF16)
            blocks = jnp.concatenate(
                [jnp.where(head_of == h, stepped_b, jnp.zeros_like(stepped_b)) for h in range(5)], axis=0
            )
            state = got[perm[s]]
            out = dot(mixing, blocks, NN)
            out += jnp.exp(cum_wide) * dot(c_s, state, NT)
            out += skip * inputs
            last = cum_wide[TOKENS - 1 : TOKENS, :]
            to_end = (jnp.exp(last - cum_wide) * stepped).astype(BF16)
            fade_high, fade_low = halves(jnp.exp(last))
            first = iota((16, WIDTH), 0)
            zero = jnp.zeros((16, WIDTH), BF16)
            fade = jnp.where(first == 0, fade_high, jnp.where(first == 1, fade_low, zero))
            carry_ref[s] = dot(fade, ones, TN) * state.astype(F32) + dot(to_end, b_s, TN)
            gate = jnp.concatenate([xz[rows, 256:512], xz[rows, 576:640]], axis=1)
            gated = out * gate * (1.0 / (1.0 + jnp.exp(-gate)))
            mean_square = jnp.sum(gated * gated, axis=1, keepdims=True) * (1.0 / WIDTH)
            both[yl, rows, :] = (gated * lax.rsqrt(mean_square + 1e-05) * gain).astype(BF16)

    def give(q):
        ref = both.at[yl, rows_at(q)]
        return remote(ref, ref, ns.at[q], nr.at[q], partner)

    def given(q):
        ref = both.at[1 - yl, rows_at(q)]
        remote(ref, ref, nr.at[q], nr.at[q], partner).wait_recv()
        bothr[rows_at(q), :] = jnp.concatenate([both[0, rows_at(q), 256:320], both[1, rows_at(q), 256:320]], axis=1)

    def term(to, q):
        at = 4 * (to // 2) + 2 * (to % 2)
        total = dot(both[0, rows_at(q), 0:256], wo[at, 0:WIDTH, :], NT)
        total += dot(both[1, rows_at(q), 0:256], wo[at + 1, 0:WIDTH, :], NT)
        total += dot(bothr[rows_at(q), :], worem[to], NT)
        return total[:, 0:256], jnp.concatenate([total[48 * g : 48 * g + 48, 256:320] for g in range(3)], axis=1)

    def relay(sign, t, q):
        if sign > 0:
            return remote(sendp.at[t, q], recvp.at[t, q], ps.at[t, q], pr.at[t, q], up)
        return remote(sendm.at[t, q], recvm.at[t, q], ms.at[t, q], mr.at[t, q], down)

    def starts(sign, q):
        return 0 if (q < 2) == (sign > 0) else 1

    def go(t, q):
        for sign in (1, -1):
            if t < starts(sign, q):
                continue
            main, rest = term((z + 8 + sign * (4 - t)) % 8, q)
            send, recv = (sendp, recvp) if sign > 0 else (sendm, recvm)
            if t > starts(sign, q):
                relay(sign, t - 1, q).wait_recv()
                main = main + recv[t - 1, q, 0:QUARTER, :].astype(F32)
                rest = rest + recv[t - 1, q, QUARTER:192, 0:192].astype(F32)
            send[t, q, 0:QUARTER, :] = main.astype(BF16)
            send[t, q, QUARTER:192, :] = jnp.concatenate([rest, jnp.zeros((48, 64), F32)], axis=1).astype(BF16)
            relay(sign, t, q).start()

    def arrive(q):
        main, rest = term(z, q)
        relay(1, 3, q).wait_recv()
        relay(-1, 3, q).wait_recv()
        for recv in (recvp, recvm):
            main = main + recv[3, q, 0:QUARTER, :].astype(F32)
            rest = rest + recv[3, q, QUARTER:192, 0:192].astype(F32)
        mixed_ref[rows_at(q), 0:256] = main.astype(BF16)
        rest = jnp.concatenate([rest[:, 64 * g : 64 * g + 64] for g in range(3)], axis=0)
        mixed_ref[rows_at(q), 256:320] = rest.astype(BF16)

    scan(0)
    give(0).start()
    scan(1)
    give(1).start()
    for ys in range(4):
        stage_last(1, ys)
    finish(1)

    @pl.loop(0, 8)
    def _(d):
        at = 4 * (d // 2) + 2 * (d % 2)
        for b in range(2):
            for g in range(4):
                worem[d, 80 * g : 80 * g + 80, 64 * b : 64 * b + 64] = wo[at + b, WIDTH : WIDTH + 80, 64 * g : 64 * g + 64]

    given(0)
    go(0, 0)
    scan(2)
    give(2).start()
    given(1)
    go(0, 1)
    go(1, 0)
    scan(3)
    give(3).start()
    go(1, 1)
    given(2)
    go(0, 2)
    go(2, 0)
    given(3)
    go(0, 3)
    go(1, 2)
    go(2, 1)
    go(3, 0)
    go(1, 3)
    go(2, 2)
    go(3, 1)
    go(2, 3)
    arrive(0)
    go(3, 2)
    arrive(1)
    go(3, 3)
    arrive(2)
    arrive(3)

    for q in range(4):
        give(q).wait_send()
        for sign in (1, -1):
            for t in range(starts(sign, q), 4):
                relay(sign, t, q).wait_send()
        swap(q).wait_send()
    for i in range(7):
        mixes(i).wait_send()
    for t in range(4):
        for g in range(3):
            ring(t, 1, g).wait_send()
            ring(t, -1, g).wait_send()


def layer(moved, bias, rate, skip, win, wout, side, xmask, omask, xrows, kept, gain):
    vmem = pl.BlockSpec(memory_space=pltpu.VMEM)
    smem = pl.BlockSpec(memory_space=pltpu.SMEM)
    dma = pltpu.SemaphoreType.DMA
    return pl.pallas_call(
        layer_kernel,
        out_shape=(
            jax.ShapeDtypeStruct((ROWS, WIDTH), BF16),
            jax.ShapeDtypeStruct((SLOTS, WIDTH, NSTATE), F32),
        ),
        in_specs=[smem] * 4 + [vmem] * 8,
        out_specs=(vmem, vmem),
        scratch_shapes=[
            pltpu.VMEM((WIDTH, WIDE), BF16),
            pltpu.VMEM((PACKED, 256), BF16),
            pltpu.VMEM((SIDE, WIDTH), BF16),
            pltpu.VMEM((16, WIDTH, WIDE), BF16),
            pltpu.VMEM((16, PACKED, 256), BF16),
            pltpu.VMEM((8, WIDTH, 128), BF16),
            pltpu.VMEM((16, SIDE, WIDTH), BF16),
            pltpu.VMEM((2, 512, WIDE), BF16),
            pltpu.VMEM((2, 2, SIDE, 256), BF16),
            pltpu.VMEM((8, ROWS, 256), BF16),
            pltpu.VMEM((8, 288, 128), BF16),
            pltpu.VMEM((2, ROWS, 256), BF16),
            pltpu.VMEM((SLOTS, WIDTH, NSTATE), BF16),
            pltpu.VMEM((8, 128), jnp.int32),
            pltpu.VMEM((MOST, WIDTH, NSTATE), BF16),
            pltpu.VMEM((8, 128), jnp.int32),
            pltpu.VMEM((SLOTS, WIDTH, NSTATE), BF16),
            pltpu.VMEM((4, 8, 128), jnp.int32),
            pltpu.SMEM((4, 8, 128), jnp.int32),
            pltpu.SMEM((SLOTS,), jnp.int32),
            pltpu.VMEM((ROWS, WIDE), F32),
            pltpu.VMEM((ROWS, WIDE), BF16),
            pltpu.VMEM((ROWS, WIDE), BF16),
            pltpu.VMEM((SIDE, ROWS), BF16),
            pltpu.VMEM((SIDE, ROWS), BF16),
            pltpu.VMEM((MIXES, 640), BF16),
            pltpu.VMEM((8, MIXES, 640), BF16),
            pltpu.VMEM((128, 640), F32),
            pltpu.VMEM((640, NSTATE), BF16),
            pltpu.VMEM((640, NSTATE), BF16),
            pltpu.VMEM((640, 128), F32),
            pltpu.VMEM((2, ROWS, WIDTH), BF16),
            pltpu.VMEM((ROWS, 128), BF16),
        ]
        + [pltpu.VMEM((4, 4, 192, 256), BF16)] * 4
        + [dma((3, 4))] * 8
        + [dma((3, 16))] * 2
        + [dma((4, 3))] * 4
        + [dma((4,))] * 4
        + [dma((4,))] * 2
        + [dma((7,))] * 2
        + [dma((4,))] * 2
        + [dma((4, 4))] * 4
        + [dma] * 3
        + [dma((2,))] * 2,
        compiler_params=pltpu.CompilerParams(
            collective_id=0, has_side_effects=True, vmem_limit_bytes=58 * 1024 * 1024
        ),
        name="layer",
    )(moved, bias, rate, skip, win, wout, side, xmask, omask, xrows, kept, gain)


def on_device(
    frames_in,
    kept_state,
    moved_to,
    xz_weight,
    side_weight,
    xz_mask,
    dt_bias,
    decay_rate,
    skip_gain,
    norm_gain,
    out_weight,
    out_mask,
):
    mixed, carry = layer(
        moved_to,
        dt_bias,
        decay_rate,
        skip_gain,
        xz_weight,
        out_weight,
        side_weight,
        xz_mask,
        out_mask,
        frames_in.transpose(0, 2, 1, 3).reshape(ROWS, WIDTH),
        kept_state.reshape(SLOTS, WIDTH, NSTATE),
        norm_gain,
    )
    return (
        mixed.reshape(SLOTS, TOKENS // FRAMES, FRAMES, WIDTH).transpose(0, 2, 1, 3),
        carry.reshape(SLOTS, 5, 64, NSTATE),
    )


def solution(mesh):
    placed = (
        P("stream", None, None, "shard"),
        P("stream", "shard", None, None),
        P("stream"),
        P("stream", None, "shard"),
        P("stream", None),
        P(),
        P("shard"),
        P("shard"),
        P("shard"),
        P("shard"),
        P("stream", "shard"),
        P(),
    )
    return jax.shard_map(
        on_device,
        mesh=mesh,
        in_specs=placed,
        out_specs=(P("stream", None, None, "shard"), P("stream", "shard", None, None)),
        check_vma=False,
    )
```

```python
import jax
import jax.numpy as jnp
from jax import lax
from jax.experimental import pallas as pl
from jax.experimental.pallas import tpu as pltpu
from jax.sharding import PartitionSpec as P

MESH = pl.DeviceIdType.MESH
F32, BF16 = jnp.float32, jnp.bfloat16

NSTATE = 128
BLOCK = 128
FRAMES = 4
MOST = 3
HOPS = (1, 2, 3, 8)
ROWS = 576
SLOTS = 12
TOKENS = 48
WIDTH = 320
WIDE = 640
COLUMNS = (slice(0, 256), slice(256, 512), slice(512, 640))
MIXES = 32
SIDE = 64
SIDE_AT = 32
PACKED = 416
QUARTER = 144
NT, NN, TN = ((1,), (1,)), ((1,), (0,)), ((0,), (0,))


def place():
    si, ki = lax.axis_index("stream"), lax.axis_index("shard")
    return si // 4, (si // 2) % 2, si % 2, ki // 2, ki % 2


def device(x, y, c, z):
    return {"stream": 4 * x + 2 * (y // 2) + c, "shard": 2 * z + y % 2}


def remote(src, dst, send, recv, where):
    return pltpu.make_async_remote_copy(
        src_ref=src, dst_ref=dst, send_sem=send, recv_sem=recv, device_id=where, device_id_type=MESH
    )


def dot(a, b, dims):
    return lax.dot_general(a, b, (dims, ((), ())), preferred_element_type=F32)


def iota(shape, axis):
    return lax.broadcasted_iota(jnp.int32, shape, axis)


def halves(value):
    high = value.astype(BF16)
    return high, (value - high.astype(F32)).astype(BF16)


def layer_kernel(
    moved_ref, bias_ref, rate_ref, skip_ref,
    win_ref, wout_ref, side_ref, xmask_ref, omask_ref, x_ref, kept_ref, gain_ref,
    mixed_ref, carry_ref,
    w1, w2, ws, wg, wo, worem, wsg, wrem, wsr, xm, xr, xk, st, sl, st8, sl8, got, gsl, gsl_s, perm,
    xz, psend, precv, ssend, srecv, bct, bc, tile, mix_in, mix_out, steps,
    both, bothr, sendp, recvp, sendm, recvm,
    ysend, yrecv, xps, xpr, xms, xmr, x2s, x2r, ss, sr,
    zps, zpr, zms, zmr, sts, strv, sls, slr, psn, prc, bcs, bcr,
    ns, nr, ps, pr, ms, mr, local, sps, spr, rls, rlr,
):
    x, yh, c, z, yl = place()
    y = 2 * yh + yl
    si, ki = lax.axis_index("stream"), lax.axis_index("shard")
    here = 4 * x + y
    xrt, xlt = (x + 1) % 4, (x + 3) % 4
    up = {"stream": si, "shard": 2 * ((z + 1) % 8) + yl}
    down = {"stream": si, "shard": 2 * ((z + 7) % 8) + yl}
    partner = {"stream": si, "shard": 2 * z + 1 - yl}
    peer = device(x, y, 1 - c, z)

    barrier = pltpu.get_barrier_semaphore()

    @pl.loop(1, 32)
    def _(i):
        other = (si * 2 + yl + i) % 32
        pl.semaphore_signal(
            barrier, inc=1, device_id={"stream": other // 2, "shard": 2 * z + other % 2}, device_id_type=MESH
        )

    @pl.loop(1, 8)
    def _(i):
        pl.semaphore_signal(
            barrier, inc=1, device_id={"stream": si, "shard": 2 * ((z + i) % 8) + yl}, device_id_type=MESH
        )

    tokens = x_ref[...].reshape(ROWS, WIDTH)
    xm[z] = tokens[:, 0:256]
    xr[z] = jnp.concatenate([tokens[0:288, 256:320], tokens[288:576, 256:320]], axis=1)

    rows_of = (iota((WIDTH, 40), 1) == (si * WIDTH + iota((WIDTH, 40), 0)) // BLOCK).astype(BF16)
    cols_of = (iota((40, WIDTH), 0) == (ki * WIDTH + iota((40, WIDTH), 1)) // BLOCK).astype(BF16)

    def keep(mask):
        return dot(dot(rows_of, mask.astype(F32).astype(BF16), NN).astype(BF16), cols_of, NN).astype(BF16)

    pick, pick_row = iota((SIDE, 336), 0), iota((SIDE, 336), 1)
    chosen = jnp.where(pick < MIXES, pick + MIXES * z, pick - MIXES + 2 * NSTATE + 5 * ki)
    chosen = (pick_row == chosen) & (pick < MIXES + 5)
    ws[...] = dot(chosen.astype(F32).astype(BF16), side_ref[...], NT).astype(BF16)
    inner, gates = win_ref[:, 0, :] * keep(xmask_ref[:, 0, :]), win_ref[:, 1, :] * keep(xmask_ref[:, 1, :])
    w1[:, 0:256] = inner[:, 0:256]
    w1[:, 256:512] = gates[:, 0:256]
    w1[:, 512:640] = jnp.concatenate([inner[:, 256:320], gates[:, 256:320]], axis=1)

    pl.semaphore_wait(barrier, 38)

    pairs = ((w1, wg), (w2, wo), (ws, wsg))
    sizes = (WIDTH // 2, PACKED // 2, SIDE // 2)

    def half(w, core):
        return pl.ds(pl.multiple_of(core * sizes[w], sizes[w]), sizes[w])

    def y_copies(w):
        own, full = pairs[w]
        for a in range(2):
            for h in range(2):
                part = pl.ds(h * sizes[w], sizes[w])
                to = c + 2 * a
                mine = (to == y) & (c == h)
                yield mine, remote(
                    own.at[part], full.at[here, part], ysend.at[w, 2 * a + h], yrecv.at[w, y], device(x, to, h, z)
                ), pltpu.make_async_copy(own.at[part], full.at[here, part], yrecv.at[w, y])

    def y_start(w):
        for mine, far, near in y_copies(w):
            @pl.when(mine)
            def _():
                near.start()

            @pl.when(jnp.logical_not(mine))
            def _():
                far.start()

    def y_finish(w):
        for mine, far, near in y_copies(w):
            @pl.when(jnp.logical_not(mine))
            def _():
                far.wait_send()

    def block(w, x_of, ys, core=c):
        return pairs[w][1].at[4 * x_of + ys, half(w, core)]

    def hop(w, x_of, ys, send, recv, x_to):
        ref = block(w, x_of, ys)
        return remote(ref, ref, send.at[w, ys], recv.at[w, ys], device(x_to, y, c, z))

    def sibling(w, q, x_of, ys):
        ref = block(w, x_of, ys)
        return remote(ref, ref, ss.at[w, 4 * q + ys], sr.at[w, 4 * q + ys], peer)

    def landed(w, x_of, ys, recv):
        ref = block(w, x_of, ys)
        remote(ref, ref, recv.at[w, ys], recv.at[w, ys], peer).wait_recv()

    def stage_x(w, ys):
        landed(w, x, ys, yrecv)
        hop(w, x, ys, xps, xpr, xrt).start()
        hop(w, x, ys, xms, xmr, xlt).start()
        sibling(w, 0, x, ys).start()

    def stage_far(w, ys):
        landed(w, xlt, ys, xpr)
        if ys < 2:
            hop(w, xlt, ys, x2s, x2r, xrt).start()
        sibling(w, 1, xlt, ys).start()
        landed(w, xrt, ys, xmr)
        if ys >= 2:
            hop(w, xrt, ys, x2s, x2r, xlt).start()
        sibling(w, 2, xrt, ys).start()

    def stage_last(w, ys):
        landed(w, (x + 2) % 4, ys, x2r)
        sibling(w, 3, (x + 2) % 4, ys).start()

    def finish(w):
        y_finish(w)
        for q, x_of in enumerate((x, xlt, xrt, (x + 2) % 4)):
            for ys in range(4):
                sibling(w, q, x_of, ys).wait_send()
                ref = block(w, x_of, ys, 1 - c)
                remote(ref, ref, sr.at[w, 4 * q + ys], sr.at[w, 4 * q + ys], peer).wait_recv()
        for ys in range(4):
            hop(w, x, ys, xps, xpr, xrt).wait_send()
            hop(w, x, ys, xms, xmr, xlt).wait_send()
            hop(w, xlt if ys < 2 else xrt, ys, x2s, x2r, xrt if ys < 2 else xlt).wait_send()

    def piece(t, sign, g, src):
        if g == 2:
            part = pl.ds(0, 288) if t < 3 else pl.ds(0 if sign > 0 else 144, 144)
            return xr.at[src, part]
        if t < 3:
            return xm.at[src, pl.ds(288 * g, 288)]
        return xm.at[src, pl.ds((0 if sign > 0 else 288) + 144 * g, 144)]

    def ring(t, sign, g):
        ref = piece(t, sign, g, (z - sign * t + 8) % 8)
        if sign > 0:
            return remote(ref, ref, zps.at[t, g], zpr.at[t, g], up)
        return remote(ref, ref, zms.at[t, g], zmr.at[t, g], down)

    def ring_start(t):
        for g in range(3):
            for sign in (1, -1):
                if 0 < t < 3:
                    ring_land(t - 1, sign, g)
                ring(t, sign, g).start()

    def ring_land(t, sign, g):
        ref = piece(t, sign, g, (z - sign * (t + 1) + 8) % 8)
        sem = zpr if sign > 0 else zmr
        remote(ref, ref, sem.at[t, g], sem.at[t, g], up).wait_recv()

    def states():
        for t, hops in enumerate(HOPS[:3]):
            where = {"stream": (si + hops) % 16, "shard": ki}
            yield remote(st.at[pl.ds(MOST * t, MOST)], got.at[pl.ds(MOST * t, MOST)], sts.at[t], strv.at[t], where)
            yield remote(sl, gsl.at[t], sls.at[t], slr.at[t], where)

    def relays():
        where = {"stream": (si + 12) % 16, "shard": ki}
        part = pl.ds(3 * MOST, MOST)
        first = remote(st.at[part], st8, rls.at[0], rlr.at[0], where), remote(sl, sl8, rls.at[1], rlr.at[1], where)
        last = remote(st8, got.at[part], sts.at[3], strv.at[3], where), remote(sl8, gsl.at[3], sls.at[3], slr.at[3], where)
        return first, last

    y_start(2)
    y_start(0)
    ring_start(0)
    outer = wout_ref[...] * keep(omask_ref[...])
    w2[0:WIDTH, :] = outer[:, 0:256]
    w2[WIDTH : WIDTH + 80, :] = jnp.concatenate([outer[80 * g : 80 * g + 80, 256:320] for g in range(4)], axis=1)
    w2[WIDTH + 80 : PACKED, :] = jnp.zeros((16, 256), BF16)
    y_start(1)
    for ys in range(4):
        stage_x(2, ys)
    stage_x(0, 0)
    stage_x(0, 1)

    ways = [jnp.minimum((moved_ref[j] // SLOTS - si + 16) % 16 - 1, 3) for j in range(SLOTS)]
    spots = []
    for j in range(SLOTS):
        rank = sum(((ways[i] == ways[j]).astype(jnp.int32) for i in range(j)), jnp.int32(0))
        spots.append(MOST * ways[j] + rank)
    lane = iota((8, 128), 1)
    slots = jnp.zeros((8, 128), jnp.int32)
    for j in range(SLOTS):
        slots = jnp.where(lane == spots[j], moved_ref[j] % SLOTS, slots)
    sl[...] = slots
    stage_x(0, 2)
    stage_x(0, 3)
    for p in range(SLOTS):
        source = sum((jnp.where(spots[j] == p, j, 0) for j in range(1, SLOTS)), jnp.int32(0))
        st[p] = kept_ref[jnp.minimum(source, SLOTS - 1)].astype(BF16)
    ring_start(1)
    for ys in range(4):
        stage_far(2, ys)
    stage_far(0, 0)
    stage_far(0, 1)
    ring_start(2)
    for ys in range(4):
        stage_last(2, ys)
    for copy in states():
        copy.start()
    stage_far(0, 2)
    stage_far(0, 3)
    to_relay, relayed = relays()
    for copy in to_relay:
        copy.start()
    for g in range(3):
        for sign in (1, -1):
            ring_land(2, sign, g)
    ring_start(3)
    finish(2)
    stage_last(0, 0)
    stage_last(0, 1)
    for j in range(8):
        for b in range(2):
            lanes = slice(64 * (j % 4), 64 * (j % 4) + 64)
            wsr[b, j // 4, :, lanes] = wsg[4 * (j // 2) + 2 * (j % 2) + b, :, 256:320]
    tile[...] = jnp.zeros_like(tile)
    for g in range(3):
        for sign in (1, -1):
            ring_land(3, sign, g)

    low = iota((288, 128), 1) < 64
    for i in range(4):
        first, second = xr[2 * i].astype(F32), xr[2 * i + 1].astype(F32)
        lanes = slice(128 * (i % 2), 128 * (i % 2) + 128)
        xk[i // 2, 0:288, lanes] = jnp.where(low, first, pltpu.roll(second, 64, 1)).astype(BF16)
        xk[i // 2, 288:576, lanes] = jnp.where(low, pltpu.roll(first, 64, 1), second).astype(BF16)

    def side_sums(b):
        total = None
        for j in range(8):
            one = dot(wsg[4 * (j // 2) + 2 * (j % 2) + b, :, 0:256], xm[j], NT)
            total = one if total is None else total + one
        for i in range(2):
            total = total + dot(wsr[b, i], xk[i], NT)
        return total

    def mixes(i):
        return remote(bct, bc.at[z], bcs.at[i], bcr.at[i], {"stream": si, "shard": 2 * ((z + i + 1) % 8) + yl})

    ssend[...] = side_sums(1 - yl).astype(BF16)
    side_swap = remote(ssend, srecv, sps, spr, partner)
    side_swap.start()
    tile[0:SIDE, 0:ROWS] = side_sums(yl)
    for copy in to_relay:
        copy.wait_recv()
    for copy in relayed:
        copy.start()
    stage_last(0, 2)
    stage_last(0, 3)
    side_swap.wait()
    tile[0:SIDE, 0:ROWS] += srecv[...].astype(F32)
    bct[...] = tile[0:MIXES, :].astype(BF16)
    bc[z] = bct[...]
    for i in range(7):
        mixes(i).start()
    for ys in range(4):
        stage_x(1, ys)

    finish(0)
    for j in range(8):
        for b in range(2):
            wrem[b, 64 * j : 64 * j + 64, :] = wg[4 * (j // 2) + 2 * (j % 2) + b, 256:320, :]

    def matmul(b, n, r):
        rows = slice(288 * r, 288 * r + 288)
        total = None
        for j in range(8):
            one = dot(xm[j, rows, :], wg[4 * (j // 2) + 2 * (j % 2) + b, 0:256, COLUMNS[n]], NN)
            total = one if total is None else total + one
        for i in range(2):
            total = total + dot(xk[i, rows, :], wrem[b, 256 * i : 256 * i + 256, COLUMNS[n]], NN)
        return total

    def rows_at(q):
        return pl.ds(QUARTER * q, QUARTER)

    def swap(q):
        return remote(psend.at[rows_at(q)], precv.at[rows_at(q)], psn.at[q], prc.at[q], partner)

    for r in range(2):
        for n in range(3):
            psend[288 * r : 288 * r + 288, COLUMNS[n]] = matmul(1 - yl, n, r).astype(BF16)
        if r == 0:
            swap(0).start()
            swap(1).start()
    for r in range(2):
        for n in range(3):
            xz[288 * r : 288 * r + 288, COLUMNS[n]] = matmul(yl, n, r)

    for ys in range(4):
        stage_far(1, ys)

    for copy in states():
        copy.wait()
    for copy in relayed:
        copy.wait()
    for copy in to_relay:
        copy.wait_send()
    fetch = pltpu.make_async_copy(gsl, gsl_s, local)
    fetch.start()
    raw_bias = jnp.zeros((1, 128), F32)
    rate = jnp.zeros((1, 128), F32)
    skip = jnp.zeros((1, WIDTH), F32)
    for h in range(5):
        raw_bias = jnp.where(iota((1, 128), 1) == SIDE_AT + h, bias_ref[h], raw_bias)
        rate = jnp.where(iota((1, 128), 1) == SIDE_AT + h, rate_ref[h], rate)
        skip = jnp.where(iota((1, WIDTH), 1) // 64 == h, skip_ref[h], skip)
    gain = gain_ref[...].reshape(1, WIDTH)
    raw = tile[...].T + raw_bias
    live = (iota((1, 128), 1) >= SIDE_AT) & (iota((1, 128), 1) < SIDE_AT + 5)
    steps[...] = jnp.where(live, jnp.maximum(raw, 0.0) + jnp.log1p(jnp.exp(-jnp.abs(raw))), 0.0)
    fetch.wait()
    landing = [gsl_s[j // MOST, 0, j] for j in range(SLOTS)]
    for s in range(SLOTS):
        found = sum((jnp.where(landing[j] == s, j, 0) for j in range(1, SLOTS)), jnp.int32(0))
        perm[s] = jnp.minimum(found, SLOTS - 1)

    spread = jnp.concatenate(
        [
            iota((128, 384), 0) == SIDE_AT + iota((128, 384), 1) // 64,
            (iota((128, 256), 0) == SIDE_AT + iota((128, 256), 1) // TOKENS) & (iota((128, 256), 1) < 240),
        ],
        axis=1,
    ).astype(F32).astype(BF16)
    spread = jnp.concatenate([spread, spread], axis=0)
    def time(row):
        return (row % FRAMES) * (TOKENS // FRAMES) + row // FRAMES

    in_order = time(iota((TOKENS, TOKENS), 0)) >= time(iota((TOKENS, TOKENS), 1))
    lower = in_order.astype(F32).astype(BF16)
    token_of = iota((TOKENS, 240), 1) % TOKENS
    causal = time(iota((TOKENS, 240), 0)) >= time(token_of)
    same = iota((TOKENS, 240), 0) == token_of
    head_of = iota((TOKENS, WIDTH), 1) // 64
    ones = jnp.ones((16, NSTATE), BF16)

    for i in range(7):
        src = (z + 7 - i) % 8
        remote(bct, bc.at[src], bcr.at[i], bcr.at[i], partner).wait_recv()
    mix_in[...] = bc[0:4].reshape(NSTATE, 640).astype(F32).T.astype(BF16)
    mix_out[...] = bc[4:8].reshape(NSTATE, 640).astype(F32).T.astype(BF16)

    def scan(q):
        swap(q).wait_recv()
        xz[rows_at(q), :] += precv[rows_at(q), :].astype(F32)

        @pl.loop(0, 3)
        def _(i):
            s = 3 * q + i
            rows = pl.ds(pl.multiple_of(s * TOKENS, TOKENS), TOKENS)
            step = steps[rows, :]
            step_parts = halves(step)
            decay_parts = halves(-rate * step)
            cumulative = dot(lower, decay_parts[0], NN) + dot(lower, decay_parts[1], NN)
            cum_all = dot(jnp.concatenate(halves(cumulative), axis=1), spread, NN)
            step_wide = dot(jnp.concatenate(step_parts, axis=1), spread[:, 0:384], NN)[:, 0:WIDTH]
            cum_wide = cum_all[:, 0:WIDTH]
            cum_left = cum_all[:, 384:624]
            cum_right = jnp.sum(jnp.where(same, cum_left, 0.0), axis=0, keepdims=True)
            b_s, c_s = mix_in[rows, :], mix_out[rows, :]
            scores = dot(c_s, jnp.concatenate([b_s] * 5, axis=0), NT)
            mixing = jnp.where(causal, jnp.exp(jnp.where(causal, cum_left - cum_right, 0.0)) * scores, 0.0).astype(BF16)
            inputs = jnp.concatenate([xz[rows, 0:256], xz[rows, 512:576]], axis=1)
            stepped = inputs * step_wide
            stepped_b = stepped.astype(BF16)
            blocks = jnp.concatenate(
                [jnp.where(head_of == h, stepped_b, jnp.zeros_like(stepped_b)) for h in range(5)], axis=0
            )
            state = got[perm[s]]
            out = dot(mixing, blocks, NN)
            out += jnp.exp(cum_wide) * dot(c_s, state, NT)
            out += skip * inputs
            last = cum_wide[TOKENS - 1 : TOKENS, :]
            to_end = (jnp.exp(last - cum_wide) * stepped).astype(BF16)
            fade_high, fade_low = halves(jnp.exp(last))
            first = iota((16, WIDTH), 0)
            zero = jnp.zeros((16, WIDTH), BF16)
            fade = jnp.where(first == 0, fade_high, jnp.where(first == 1, fade_low, zero))
            carry_ref[s] = dot(fade, ones, TN) * state.astype(F32) + dot(to_end, b_s, TN)
            gate = jnp.concatenate([xz[rows, 256:512], xz[rows, 576:640]], axis=1)
            gated = out * gate * (1.0 / (1.0 + jnp.exp(-gate)))
            mean_square = jnp.sum(gated * gated, axis=1, keepdims=True) * (1.0 / WIDTH)
            both[yl, rows, :] = (gated * lax.rsqrt(mean_square + 1e-05) * gain).astype(BF16)

    def give(q):
        ref = both.at[yl, rows_at(q)]
        return remote(ref, ref, ns.at[q], nr.at[q], partner)

    def given(q):
        ref = both.at[1 - yl, rows_at(q)]
        remote(ref, ref, nr.at[q], nr.at[q], partner).wait_recv()
        bothr[rows_at(q), :] = jnp.concatenate([both[0, rows_at(q), 256:320], both[1, rows_at(q), 256:320]], axis=1)

    def term(to, q):
        at = 4 * (to // 2) + 2 * (to % 2)
        total = dot(both[0, rows_at(q), 0:256], wo[at, 0:WIDTH, :], NT)
        total += dot(both[1, rows_at(q), 0:256], wo[at + 1, 0:WIDTH, :], NT)
        total += dot(bothr[rows_at(q), :], worem[to], NT)
        return total[:, 0:256], jnp.concatenate([total[48 * g : 48 * g + 48, 256:320] for g in range(3)], axis=1)

    def relay(sign, t, q):
        if sign > 0:
            return remote(sendp.at[t, q], recvp.at[t, q], ps.at[t, q], pr.at[t, q], up)
        return remote(sendm.at[t, q], recvm.at[t, q], ms.at[t, q], mr.at[t, q], down)

    def starts(sign, q):
        return 0 if (q < 2) == (sign > 0) else 1

    def go(t, q):
        for sign in (1, -1):
            if t < starts(sign, q):
                continue
            main, rest = term((z + 8 + sign * (4 - t)) % 8, q)
            send, recv = (sendp, recvp) if sign > 0 else (sendm, recvm)
            if t > starts(sign, q):
                relay(sign, t - 1, q).wait_recv()
                main = main + recv[t - 1, q, 0:QUARTER, :].astype(F32)
                rest = rest + recv[t - 1, q, QUARTER:192, 0:192].astype(F32)
            send[t, q, 0:QUARTER, :] = main.astype(BF16)
            send[t, q, QUARTER:192, :] = jnp.concatenate([rest, jnp.zeros((48, 64), F32)], axis=1).astype(BF16)
            relay(sign, t, q).start()

    def arrive(q):
        main, rest = term(z, q)
        relay(1, 3, q).wait_recv()
        relay(-1, 3, q).wait_recv()
        for recv in (recvp, recvm):
            main = main + recv[3, q, 0:QUARTER, :].astype(F32)
            rest = rest + recv[3, q, QUARTER:192, 0:192].astype(F32)
        rest = jnp.concatenate([rest[:, 64 * g : 64 * g + 64] for g in range(3)], axis=0)
        whole = jnp.concatenate([main, rest], axis=1)
        mixed_ref[pl.ds(36 * q, 36)] = whole.reshape(36, FRAMES, WIDTH).astype(BF16)

    scan(0)
    give(0).start()
    swap(2).start()
    scan(1)
    give(1).start()
    swap(3).start()
    for ys in range(4):
        stage_last(1, ys)
    finish(1)

    @pl.loop(0, 8)
    def _(d):
        at = 4 * (d // 2) + 2 * (d % 2)
        for b in range(2):
            for g in range(4):
                worem[d, 80 * g : 80 * g + 80, 64 * b : 64 * b + 64] = wo[at + b, WIDTH : WIDTH + 80, 64 * g : 64 * g + 64]

    given(0)
    go(0, 0)
    scan(2)
    give(2).start()
    given(1)
    go(0, 1)
    go(1, 0)
    scan(3)
    give(3).start()
    go(1, 1)
    given(2)
    go(0, 2)
    go(2, 0)
    given(3)
    go(0, 3)
    go(1, 2)
    go(2, 1)
    go(3, 0)
    go(1, 3)
    go(2, 2)
    go(3, 1)
    go(2, 3)
    arrive(0)
    go(3, 2)
    arrive(1)
    go(3, 3)
    arrive(2)
    arrive(3)

    for q in range(4):
        give(q).wait_send()
        for sign in (1, -1):
            for t in range(starts(sign, q), 4):
                relay(sign, t, q).wait_send()
        swap(q).wait_send()
    for i in range(7):
        mixes(i).wait_send()
    for t in range(4):
        for g in range(3):
            ring(t, 1, g).wait_send()
            ring(t, -1, g).wait_send()


def layer(moved, bias, rate, skip, win, wout, side, xmask, omask, xrows, kept, gain):
    vmem = pl.BlockSpec(memory_space=pltpu.VMEM)
    smem = pl.BlockSpec(memory_space=pltpu.SMEM)
    dma = pltpu.SemaphoreType.DMA
    return pl.pallas_call(
        layer_kernel,
        out_shape=(
            jax.ShapeDtypeStruct((QUARTER, FRAMES, WIDTH), BF16),
            jax.ShapeDtypeStruct((SLOTS, WIDTH, NSTATE), F32),
        ),
        in_specs=[smem] * 4 + [vmem] * 8,
        out_specs=(vmem, vmem),
        scratch_shapes=[
            pltpu.VMEM((WIDTH, WIDE), BF16),
            pltpu.VMEM((PACKED, 256), BF16),
            pltpu.VMEM((SIDE, WIDTH), BF16),
            pltpu.VMEM((16, WIDTH, WIDE), BF16),
            pltpu.VMEM((16, PACKED, 256), BF16),
            pltpu.VMEM((8, WIDTH, 128), BF16),
            pltpu.VMEM((16, SIDE, WIDTH), BF16),
            pltpu.VMEM((2, 512, WIDE), BF16),
            pltpu.VMEM((2, 2, SIDE, 256), BF16),
            pltpu.VMEM((8, ROWS, 256), BF16),
            pltpu.VMEM((8, 288, 128), BF16),
            pltpu.VMEM((2, ROWS, 256), BF16),
            pltpu.VMEM((SLOTS, WIDTH, NSTATE), BF16),
            pltpu.VMEM((8, 128), jnp.int32),
            pltpu.VMEM((MOST, WIDTH, NSTATE), BF16),
            pltpu.VMEM((8, 128), jnp.int32),
            pltpu.VMEM((SLOTS, WIDTH, NSTATE), BF16),
            pltpu.VMEM((4, 8, 128), jnp.int32),
            pltpu.SMEM((4, 8, 128), jnp.int32),
            pltpu.SMEM((SLOTS,), jnp.int32),
            pltpu.VMEM((ROWS, WIDE), F32),
            pltpu.VMEM((ROWS, WIDE), BF16),
            pltpu.VMEM((ROWS, WIDE), BF16),
            pltpu.VMEM((SIDE, ROWS), BF16),
            pltpu.VMEM((SIDE, ROWS), BF16),
            pltpu.VMEM((MIXES, 640), BF16),
            pltpu.VMEM((8, MIXES, 640), BF16),
            pltpu.VMEM((128, 640), F32),
            pltpu.VMEM((640, NSTATE), BF16),
            pltpu.VMEM((640, NSTATE), BF16),
            pltpu.VMEM((640, 128), F32),
            pltpu.VMEM((2, ROWS, WIDTH), BF16),
            pltpu.VMEM((ROWS, 128), BF16),
        ]
        + [pltpu.VMEM((4, 4, 192, 256), BF16)] * 4
        + [dma((3, 4))] * 8
        + [dma((3, 16))] * 2
        + [dma((4, 3))] * 4
        + [dma((4,))] * 4
        + [dma((4,))] * 2
        + [dma((7,))] * 2
        + [dma((4,))] * 2
        + [dma((4, 4))] * 4
        + [dma] * 3
        + [dma((2,))] * 2,
        compiler_params=pltpu.CompilerParams(
            collective_id=0, has_side_effects=True, vmem_limit_bytes=58 * 1024 * 1024
        ),
        name="layer",
    )(moved, bias, rate, skip, win, wout, side, xmask, omask, xrows, kept, gain)


def on_device(
    frames_in,
    kept_state,
    moved_to,
    xz_weight,
    side_weight,
    xz_mask,
    dt_bias,
    decay_rate,
    skip_gain,
    norm_gain,
    out_weight,
    out_mask,
):
    mixed, carry = layer(
        moved_to,
        dt_bias,
        decay_rate,
        skip_gain,
        xz_weight,
        out_weight,
        side_weight,
        xz_mask,
        out_mask,
        frames_in.transpose(0, 2, 1, 3).reshape(QUARTER, FRAMES, WIDTH),
        kept_state.reshape(SLOTS, WIDTH, NSTATE),
        norm_gain,
    )
    return (
        mixed.reshape(SLOTS, TOKENS // FRAMES, FRAMES, WIDTH).transpose(0, 2, 1, 3),
        carry.reshape(SLOTS, 5, 64, NSTATE),
    )


def solution(mesh):
    placed = (
        P("stream", None, None, "shard"),
        P("stream", "shard", None, None),
        P("stream"),
        P("stream", None, "shard"),
        P("stream", None),
        P(),
        P("shard"),
        P("shard"),
        P("shard"),
        P("shard"),
        P("stream", "shard"),
        P(),
    )
    return jax.shard_map(
        on_device,
        mesh=mesh,
        in_specs=placed,
        out_specs=(P("stream", None, None, "shard"), P("stream", "shard", None, None)),
        check_vma=False,
    )
```

```python
import jax
import jax.numpy as jnp
from jax import lax
from jax.experimental import pallas as pl
from jax.experimental.pallas import tpu as pltpu
from jax.sharding import PartitionSpec as P

MESH = pl.DeviceIdType.MESH
F32, BF16 = jnp.float32, jnp.bfloat16

NSTATE = 128
BLOCK = 128
FRAMES = 4
MOST = 3
HOPS = (1, 2, 3, 8)
ROWS = 576
SLOTS = 12
TOKENS = 48
WIDTH = 320
WIDE = 640
COLUMNS = (slice(0, 256), slice(256, 512), slice(512, 640))
MIXES = 32
SIDE = 64
SIDE_AT = 32
PACKED = 416
QUARTER = 144
NT, NN, TN = ((1,), (1,)), ((1,), (0,)), ((0,), (0,))


def place():
    si, ki = lax.axis_index("stream"), lax.axis_index("shard")
    return si // 4, (si // 2) % 2, si % 2, ki // 2, ki % 2


def device(x, y, c, z):
    return {"stream": 4 * x + 2 * (y // 2) + c, "shard": 2 * z + y % 2}


def remote(src, dst, send, recv, where):
    return pltpu.make_async_remote_copy(
        src_ref=src, dst_ref=dst, send_sem=send, recv_sem=recv, device_id=where, device_id_type=MESH
    )


def dot(a, b, dims):
    return lax.dot_general(a, b, (dims, ((), ())), preferred_element_type=F32)


def iota(shape, axis):
    return lax.broadcasted_iota(jnp.int32, shape, axis)


def halves(value):
    high = value.astype(BF16)
    return high, (value - high.astype(F32)).astype(BF16)


def layer_kernel(
    moved_ref, bias_ref, rate_ref, skip_ref,
    win_ref, wout_ref, side_ref, xmask_ref, omask_ref, x_ref, kept_ref, gain_ref,
    mixed_ref, carry_ref,
    w1, w2, ws, wg, wo, worem, wsg, wrem, wsr, xm, xr, xk, st, sl, st8, sl8, got, gsl, gsl_s, perm,
    xz, psend, precv, ssend, srecv, bct, bc, tile, mix_in, mix_out, steps,
    both, bothr, sendp, recvp, sendm, recvm,
    ysend, yrecv, xps, xpr, xms, xmr, x2s, x2r, ss, sr,
    zps, zpr, zms, zmr, sts, strv, sls, slr, psn, prc, bcs, bcr,
    ns, nr, ps, pr, ms, mr, local, sps, spr, rls, rlr,
):
    x, yh, c, z, yl = place()
    y = 2 * yh + yl
    si, ki = lax.axis_index("stream"), lax.axis_index("shard")
    here = 4 * x + y
    xrt, xlt = (x + 1) % 4, (x + 3) % 4
    up = {"stream": si, "shard": 2 * ((z + 1) % 8) + yl}
    down = {"stream": si, "shard": 2 * ((z + 7) % 8) + yl}
    partner = {"stream": si, "shard": 2 * z + 1 - yl}
    peer = device(x, y, 1 - c, z)

    barrier = pltpu.get_barrier_semaphore()

    @pl.loop(1, 32)
    def _(i):
        other = (si * 2 + yl + i) % 32
        pl.semaphore_signal(
            barrier, inc=1, device_id={"stream": other // 2, "shard": 2 * z + other % 2}, device_id_type=MESH
        )

    @pl.loop(1, 8)
    def _(i):
        pl.semaphore_signal(
            barrier, inc=1, device_id={"stream": si, "shard": 2 * ((z + i) % 8) + yl}, device_id_type=MESH
        )

    tokens = x_ref[...].reshape(ROWS, WIDTH)
    xm[z] = tokens[:, 0:256]
    xr[z] = jnp.concatenate([tokens[0:288, 256:320], tokens[288:576, 256:320]], axis=1)

    rows_of = (iota((WIDTH, 40), 1) == (si * WIDTH + iota((WIDTH, 40), 0)) // BLOCK).astype(BF16)
    cols_of = (iota((40, WIDTH), 0) == (ki * WIDTH + iota((40, WIDTH), 1)) // BLOCK).astype(BF16)

    def keep(mask):
        return dot(dot(rows_of, mask.astype(F32).astype(BF16), NN).astype(BF16), cols_of, NN).astype(BF16)

    pick, pick_row = iota((SIDE, 336), 0), iota((SIDE, 336), 1)
    chosen = jnp.where(pick < MIXES, pick + MIXES * z, pick - MIXES + 2 * NSTATE + 5 * ki)
    chosen = (pick_row == chosen) & (pick < MIXES + 5)
    ws[...] = dot(chosen.astype(F32).astype(BF16), side_ref[...], NT).astype(BF16)
    inner, gates = win_ref[:, 0, :] * keep(xmask_ref[:, 0, :]), win_ref[:, 1, :] * keep(xmask_ref[:, 1, :])
    w1[:, 0:256] = inner[:, 0:256]
    w1[:, 256:512] = gates[:, 0:256]
    w1[:, 512:640] = jnp.concatenate([inner[:, 256:320], gates[:, 256:320]], axis=1)

    pl.semaphore_wait(barrier, 38)

    pairs = ((w1, wg), (w2, wo), (ws, wsg))
    sizes = (WIDTH // 2, PACKED // 2, SIDE // 2)

    def half(w, core):
        return pl.ds(pl.multiple_of(core * sizes[w], sizes[w]), sizes[w])

    def y_copies(w):
        own, full = pairs[w]
        for a in range(2):
            for h in range(2):
                part = pl.ds(h * sizes[w], sizes[w])
                to = c + 2 * a
                mine = (to == y) & (c == h)
                yield mine, remote(
                    own.at[part], full.at[here, part], ysend.at[w, 2 * a + h], yrecv.at[w, y], device(x, to, h, z)
                ), pltpu.make_async_copy(own.at[part], full.at[here, part], yrecv.at[w, y])

    def y_start(w):
        for mine, far, near in y_copies(w):
            @pl.when(mine)
            def _():
                near.start()

            @pl.when(jnp.logical_not(mine))
            def _():
                far.start()

    def y_finish(w):
        for mine, far, near in y_copies(w):
            @pl.when(jnp.logical_not(mine))
            def _():
                far.wait_send()

    def block(w, x_of, ys, core=c):
        return pairs[w][1].at[4 * x_of + ys, half(w, core)]

    def hop(w, x_of, ys, send, recv, x_to):
        ref = block(w, x_of, ys)
        return remote(ref, ref, send.at[w, ys], recv.at[w, ys], device(x_to, y, c, z))

    def sibling(w, q, x_of, ys):
        ref = block(w, x_of, ys)
        return remote(ref, ref, ss.at[w, 4 * q + ys], sr.at[w, 4 * q + ys], peer)

    def landed(w, x_of, ys, recv):
        ref = block(w, x_of, ys)
        remote(ref, ref, recv.at[w, ys], recv.at[w, ys], peer).wait_recv()

    def stage_x(w, ys):
        landed(w, x, ys, yrecv)
        hop(w, x, ys, xps, xpr, xrt).start()
        hop(w, x, ys, xms, xmr, xlt).start()
        sibling(w, 0, x, ys).start()

    def stage_far(w, ys):
        landed(w, xlt, ys, xpr)
        if ys < 2:
            hop(w, xlt, ys, x2s, x2r, xrt).start()
        sibling(w, 1, xlt, ys).start()
        landed(w, xrt, ys, xmr)
        if ys >= 2:
            hop(w, xrt, ys, x2s, x2r, xlt).start()
        sibling(w, 2, xrt, ys).start()

    def stage_last(w, ys):
        landed(w, (x + 2) % 4, ys, x2r)
        sibling(w, 3, (x + 2) % 4, ys).start()

    def finish(w):
        y_finish(w)
        for q, x_of in enumerate((x, xlt, xrt, (x + 2) % 4)):
            for ys in range(4):
                sibling(w, q, x_of, ys).wait_send()
                ref = block(w, x_of, ys, 1 - c)
                remote(ref, ref, sr.at[w, 4 * q + ys], sr.at[w, 4 * q + ys], peer).wait_recv()
        for ys in range(4):
            hop(w, x, ys, xps, xpr, xrt).wait_send()
            hop(w, x, ys, xms, xmr, xlt).wait_send()
            hop(w, xlt if ys < 2 else xrt, ys, x2s, x2r, xrt if ys < 2 else xlt).wait_send()

    def piece(t, sign, g, src):
        if g == 2:
            part = pl.ds(0, 288) if t < 3 else pl.ds(0 if sign > 0 else 144, 144)
            return xr.at[src, part]
        if t < 3:
            return xm.at[src, pl.ds(288 * g, 288)]
        return xm.at[src, pl.ds((0 if sign > 0 else 288) + 144 * g, 144)]

    def ring(t, sign, g):
        ref = piece(t, sign, g, (z - sign * t + 8) % 8)
        if sign > 0:
            return remote(ref, ref, zps.at[t, g], zpr.at[t, g], up)
        return remote(ref, ref, zms.at[t, g], zmr.at[t, g], down)

    def ring_start(t):
        for g in range(3):
            for sign in (1, -1):
                if 0 < t < 3:
                    ring_land(t - 1, sign, g)
                ring(t, sign, g).start()

    def ring_land(t, sign, g):
        ref = piece(t, sign, g, (z - sign * (t + 1) + 8) % 8)
        sem = zpr if sign > 0 else zmr
        remote(ref, ref, sem.at[t, g], sem.at[t, g], up).wait_recv()

    def states():
        for t, hops in enumerate(HOPS[:3]):
            where = {"stream": (si + hops) % 16, "shard": ki}
            yield remote(st.at[pl.ds(MOST * t, MOST)], got.at[pl.ds(MOST * t, MOST)], sts.at[t], strv.at[t], where)
            yield remote(sl, gsl.at[t], sls.at[t], slr.at[t], where)

    def relays():
        where = {"stream": (si + 12) % 16, "shard": ki}
        part = pl.ds(3 * MOST, MOST)
        first = remote(st.at[part], st8, rls.at[0], rlr.at[0], where), remote(sl, sl8, rls.at[1], rlr.at[1], where)
        last = remote(st8, got.at[part], sts.at[3], strv.at[3], where), remote(sl8, gsl.at[3], sls.at[3], slr.at[3], where)
        return first, last

    y_start(2)
    y_start(0)
    ring_start(0)
    outer = wout_ref[...] * keep(omask_ref[...])
    w2[0:WIDTH, :] = outer[:, 0:256]
    w2[WIDTH : WIDTH + 80, :] = jnp.concatenate([outer[80 * g : 80 * g + 80, 256:320] for g in range(4)], axis=1)
    w2[WIDTH + 80 : PACKED, :] = jnp.zeros((16, 256), BF16)
    y_start(1)
    for ys in range(4):
        stage_x(2, ys)
    stage_x(0, 0)
    stage_x(0, 1)

    ways = [jnp.minimum((moved_ref[j] // SLOTS - si + 16) % 16 - 1, 3) for j in range(SLOTS)]
    spots = []
    for j in range(SLOTS):
        rank = sum(((ways[i] == ways[j]).astype(jnp.int32) for i in range(j)), jnp.int32(0))
        spots.append(MOST * ways[j] + rank)
    lane = iota((8, 128), 1)
    slots = jnp.zeros((8, 128), jnp.int32)
    for j in range(SLOTS):
        slots = jnp.where(lane == spots[j], moved_ref[j] % SLOTS, slots)
    sl[...] = slots
    stage_x(0, 2)
    stage_x(0, 3)
    for p in range(SLOTS):
        source = sum((jnp.where(spots[j] == p, j, 0) for j in range(1, SLOTS)), jnp.int32(0))
        st[p] = kept_ref[jnp.minimum(source, SLOTS - 1)].astype(BF16)
    ring_start(1)
    for ys in range(4):
        stage_far(2, ys)
    stage_far(0, 0)
    stage_far(0, 1)
    ring_start(2)
    for ys in range(4):
        stage_last(2, ys)
    for copy in states():
        copy.start()
    stage_far(0, 2)
    stage_far(0, 3)
    to_relay, relayed = relays()
    for copy in to_relay:
        copy.start()
    for g in range(3):
        for sign in (1, -1):
            ring_land(2, sign, g)
    ring_start(3)
    finish(2)
    stage_last(0, 0)
    stage_last(0, 1)
    for j in range(8):
        for b in range(2):
            lanes = slice(64 * (j % 4), 64 * (j % 4) + 64)
            wsr[b, j // 4, :, lanes] = wsg[4 * (j // 2) + 2 * (j % 2) + b, :, 256:320]
    tile[...] = jnp.zeros_like(tile)
    for g in range(3):
        for sign in (1, -1):
            ring_land(3, sign, g)

    low = iota((288, 128), 1) < 64
    for i in range(4):
        first, second = xr[2 * i].astype(F32), xr[2 * i + 1].astype(F32)
        lanes = slice(128 * (i % 2), 128 * (i % 2) + 128)
        xk[i // 2, 0:288, lanes] = jnp.where(low, first, pltpu.roll(second, 64, 1)).astype(BF16)
        xk[i // 2, 288:576, lanes] = jnp.where(low, pltpu.roll(first, 64, 1), second).astype(BF16)

    def side_sums(b):
        total = None
        for j in range(8):
            one = dot(wsg[4 * (j // 2) + 2 * (j % 2) + b, :, 0:256], xm[j], NT)
            total = one if total is None else total + one
        for i in range(2):
            total = total + dot(wsr[b, i], xk[i], NT)
        return total

    def mixes(i):
        return remote(bct, bc.at[z], bcs.at[i], bcr.at[i], {"stream": si, "shard": 2 * ((z + i + 1) % 8) + yl})

    ssend[...] = side_sums(1 - yl).astype(BF16)
    side_swap = remote(ssend, srecv, sps, spr, partner)
    side_swap.start()
    tile[0:SIDE, 0:ROWS] = side_sums(yl)
    for copy in to_relay:
        copy.wait_recv()
    for copy in relayed:
        copy.start()
    stage_last(0, 2)
    stage_last(0, 3)
    side_swap.wait()
    tile[0:SIDE, 0:ROWS] += srecv[...].astype(F32)
    bct[...] = tile[0:MIXES, :].astype(BF16)
    bc[z] = bct[...]
    for i in range(7):
        mixes(i).start()
    for ys in range(4):
        stage_x(1, ys)

    finish(0)
    for j in range(8):
        for b in range(2):
            wrem[b, 64 * j : 64 * j + 64, :] = wg[4 * (j // 2) + 2 * (j % 2) + b, 256:320, :]

    def matmul(b, n, r):
        rows = slice(288 * r, 288 * r + 288)
        total = None
        for j in range(8):
            one = dot(xm[j, rows, :], wg[4 * (j // 2) + 2 * (j % 2) + b, 0:256, COLUMNS[n]], NN)
            total = one if total is None else total + one
        for i in range(2):
            total = total + dot(xk[i, rows, :], wrem[b, 256 * i : 256 * i + 256, COLUMNS[n]], NN)
        return total

    def rows_at(q):
        return pl.ds(QUARTER * q, QUARTER)

    def swap(q):
        return remote(psend.at[rows_at(q)], precv.at[rows_at(q)], psn.at[q], prc.at[q], partner)

    for r in range(2):
        for n in range(3):
            psend[288 * r : 288 * r + 288, COLUMNS[n]] = matmul(1 - yl, n, r).astype(BF16)
        if r == 0:
            swap(0).start()
            swap(1).start()
    for r in range(2):
        for n in range(3):
            xz[288 * r : 288 * r + 288, COLUMNS[n]] = matmul(yl, n, r)

    for ys in range(4):
        stage_far(1, ys)

    for copy in states():
        copy.wait()
    for copy in relayed:
        copy.wait()
    for copy in to_relay:
        copy.wait_send()
    fetch = pltpu.make_async_copy(gsl, gsl_s, local)
    fetch.start()
    raw_bias = jnp.zeros((1, 128), F32)
    rate = jnp.zeros((1, 128), F32)
    skip = jnp.zeros((1, WIDTH), F32)
    for h in range(5):
        raw_bias = jnp.where(iota((1, 128), 1) == SIDE_AT + h, bias_ref[h], raw_bias)
        rate = jnp.where(iota((1, 128), 1) == SIDE_AT + h, rate_ref[h], rate)
        skip = jnp.where(iota((1, WIDTH), 1) // 64 == h, skip_ref[h], skip)
    gain = gain_ref[...].reshape(1, WIDTH)
    raw = tile[...].T + raw_bias
    live = (iota((1, 128), 1) >= SIDE_AT) & (iota((1, 128), 1) < SIDE_AT + 5)
    steps[...] = jnp.where(live, jnp.maximum(raw, 0.0) + jnp.log1p(jnp.exp(-jnp.abs(raw))), 0.0)
    fetch.wait()
    landing = [gsl_s[j // MOST, 0, j] for j in range(SLOTS)]
    for s in range(SLOTS):
        found = sum((jnp.where(landing[j] == s, j, 0) for j in range(1, SLOTS)), jnp.int32(0))
        perm[s] = jnp.minimum(found, SLOTS - 1)

    spread = jnp.concatenate(
        [
            iota((128, 384), 0) == SIDE_AT + iota((128, 384), 1) // 64,
            (iota((128, 256), 0) == SIDE_AT + iota((128, 256), 1) // TOKENS) & (iota((128, 256), 1) < 240),
        ],
        axis=1,
    ).astype(F32).astype(BF16)
    spread = jnp.concatenate([spread, spread], axis=0)
    def time(row):
        return (row % FRAMES) * (TOKENS // FRAMES) + row // FRAMES

    in_order = time(iota((TOKENS, TOKENS), 0)) >= time(iota((TOKENS, TOKENS), 1))
    lower = in_order.astype(F32).astype(BF16)
    token_of = iota((TOKENS, 240), 1) % TOKENS
    causal = time(iota((TOKENS, 240), 0)) >= time(token_of)
    same = iota((TOKENS, 240), 0) == token_of
    head_of = iota((TOKENS, WIDTH), 1) // 64
    ones = jnp.ones((16, NSTATE), BF16)

    for i in range(7):
        src = (z + 7 - i) % 8
        remote(bct, bc.at[src], bcr.at[i], bcr.at[i], partner).wait_recv()
    mix_in[...] = bc[0:4].reshape(NSTATE, 640).astype(F32).T.astype(BF16)
    mix_out[...] = bc[4:8].reshape(NSTATE, 640).astype(F32).T.astype(BF16)

    def scan(q):
        swap(q).wait_recv()
        xz[rows_at(q), :] += precv[rows_at(q), :].astype(F32)

        @pl.loop(0, 3)
        def _(i):
            s = 3 * q + i
            rows = pl.ds(pl.multiple_of(s * TOKENS, TOKENS), TOKENS)
            step = steps[rows, :]
            step_parts = halves(step)
            decay_parts = halves(-rate * step)
            cumulative = dot(lower, decay_parts[0], NN) + dot(lower, decay_parts[1], NN)
            cum_all = dot(jnp.concatenate(halves(cumulative), axis=1), spread, NN)
            step_wide = dot(jnp.concatenate(step_parts, axis=1), spread[:, 0:384], NN)[:, 0:WIDTH]
            cum_wide = cum_all[:, 0:WIDTH]
            cum_left = cum_all[:, 384:624]
            cum_right = jnp.sum(jnp.where(same, cum_left, 0.0), axis=0, keepdims=True)
            b_s, c_s = mix_in[rows, :], mix_out[rows, :]
            scores = dot(c_s, jnp.concatenate([b_s] * 5, axis=0), NT)
            mixing = jnp.where(causal, jnp.exp(jnp.where(causal, cum_left - cum_right, 0.0)) * scores, 0.0).astype(BF16)
            inputs = jnp.concatenate([xz[rows, 0:256], xz[rows, 512:576]], axis=1)
            stepped = inputs * step_wide
            stepped_b = stepped.astype(BF16)
            blocks = jnp.concatenate(
                [jnp.where(head_of == h, stepped_b, jnp.zeros_like(stepped_b)) for h in range(5)], axis=0
            )
            state = got[perm[s]]
            out = dot(mixing, blocks, NN)
            out += jnp.exp(cum_wide) * dot(c_s, state, NT)
            out += skip * inputs
            last = cum_wide[TOKENS - 1 : TOKENS, :]
            to_end = (jnp.exp(last - cum_wide) * stepped).astype(BF16)
            fade_high, fade_low = halves(jnp.exp(last))
            first = iota((16, WIDTH), 0)
            zero = jnp.zeros((16, WIDTH), BF16)
            fade = jnp.where(first == 0, fade_high, jnp.where(first == 1, fade_low, zero))
            carry_ref[s] = (dot(fade, ones, TN) * state.astype(F32) + dot(to_end, b_s, TN)).astype(BF16)
            gate = jnp.concatenate([xz[rows, 256:512], xz[rows, 576:640]], axis=1)
            gated = out * gate * (1.0 / (1.0 + jnp.exp(-gate)))
            mean_square = jnp.sum(gated * gated, axis=1, keepdims=True) * (1.0 / WIDTH)
            both[yl, rows, :] = (gated * lax.rsqrt(mean_square + 1e-05) * gain).astype(BF16)

    def give(q):
        ref = both.at[yl, rows_at(q)]
        return remote(ref, ref, ns.at[q], nr.at[q], partner)

    def given(q):
        ref = both.at[1 - yl, rows_at(q)]
        remote(ref, ref, nr.at[q], nr.at[q], partner).wait_recv()
        bothr[rows_at(q), :] = jnp.concatenate([both[0, rows_at(q), 256:320], both[1, rows_at(q), 256:320]], axis=1)

    def term(to, q):
        at = 4 * (to // 2) + 2 * (to % 2)
        total = dot(both[0, rows_at(q), 0:256], wo[at, 0:WIDTH, :], NT)
        total += dot(both[1, rows_at(q), 0:256], wo[at + 1, 0:WIDTH, :], NT)
        total += dot(bothr[rows_at(q), :], worem[to], NT)
        return total[:, 0:256], jnp.concatenate([total[48 * g : 48 * g + 48, 256:320] for g in range(3)], axis=1)

    def relay(sign, t, q):
        if sign > 0:
            return remote(sendp.at[t, q], recvp.at[t, q], ps.at[t, q], pr.at[t, q], up)
        return remote(sendm.at[t, q], recvm.at[t, q], ms.at[t, q], mr.at[t, q], down)

    def starts(sign, q):
        return 0 if (q < 2) == (sign > 0) else 1

    def go(t, q):
        for sign in (1, -1):
            if t < starts(sign, q):
                continue
            main, rest = term((z + 8 + sign * (4 - t)) % 8, q)
            send, recv = (sendp, recvp) if sign > 0 else (sendm, recvm)
            if t > starts(sign, q):
                relay(sign, t - 1, q).wait_recv()
                main = main + recv[t - 1, q, 0:QUARTER, :].astype(F32)
                rest = rest + recv[t - 1, q, QUARTER:192, 0:192].astype(F32)
            send[t, q, 0:QUARTER, :] = main.astype(BF16)
            send[t, q, QUARTER:192, :] = jnp.concatenate([rest, jnp.zeros((48, 64), F32)], axis=1).astype(BF16)
            relay(sign, t, q).start()

    def arrive(q):
        main, rest = term(z, q)
        relay(1, 3, q).wait_recv()
        relay(-1, 3, q).wait_recv()
        for recv in (recvp, recvm):
            main = main + recv[3, q, 0:QUARTER, :].astype(F32)
            rest = rest + recv[3, q, QUARTER:192, 0:192].astype(F32)
        rest = jnp.concatenate([rest[:, 64 * g : 64 * g + 64] for g in range(3)], axis=0)
        whole = jnp.concatenate([main, rest], axis=1)
        mixed_ref[pl.ds(36 * q, 36)] = whole.reshape(36, FRAMES, WIDTH).astype(BF16)

    scan(0)
    give(0).start()
    swap(2).start()
    scan(1)
    give(1).start()
    swap(3).start()
    for ys in range(4):
        stage_last(1, ys)
    finish(1)

    @pl.loop(0, 8)
    def _(d):
        at = 4 * (d // 2) + 2 * (d % 2)
        for b in range(2):
            for g in range(4):
                worem[d, 80 * g : 80 * g + 80, 64 * b : 64 * b + 64] = wo[at + b, WIDTH : WIDTH + 80, 64 * g : 64 * g + 64]

    given(0)
    go(0, 0)
    scan(2)
    give(2).start()
    given(1)
    go(0, 1)
    go(1, 0)
    scan(3)
    give(3).start()
    go(1, 1)
    given(2)
    go(0, 2)
    go(2, 0)
    given(3)
    go(0, 3)
    go(1, 2)
    go(2, 1)
    go(3, 0)
    go(1, 3)
    go(2, 2)
    go(3, 1)
    go(2, 3)
    arrive(0)
    go(3, 2)
    arrive(1)
    go(3, 3)
    arrive(2)
    arrive(3)

    for q in range(4):
        give(q).wait_send()
        for sign in (1, -1):
            for t in range(starts(sign, q), 4):
                relay(sign, t, q).wait_send()
        swap(q).wait_send()
    for i in range(7):
        mixes(i).wait_send()
    for t in range(4):
        for g in range(3):
            ring(t, 1, g).wait_send()
            ring(t, -1, g).wait_send()


def layer(moved, bias, rate, skip, win, wout, side, xmask, omask, xrows, kept, gain):
    vmem = pl.BlockSpec(memory_space=pltpu.VMEM)
    smem = pl.BlockSpec(memory_space=pltpu.SMEM)
    dma = pltpu.SemaphoreType.DMA
    return pl.pallas_call(
        layer_kernel,
        out_shape=(
            jax.ShapeDtypeStruct((QUARTER, FRAMES, WIDTH), BF16),
            jax.ShapeDtypeStruct((SLOTS, WIDTH, NSTATE), BF16),
        ),
        in_specs=[smem] * 4 + [vmem] * 8,
        out_specs=(vmem, vmem),
        scratch_shapes=[
            pltpu.VMEM((WIDTH, WIDE), BF16),
            pltpu.VMEM((PACKED, 256), BF16),
            pltpu.VMEM((SIDE, WIDTH), BF16),
            pltpu.VMEM((16, WIDTH, WIDE), BF16),
            pltpu.VMEM((16, PACKED, 256), BF16),
            pltpu.VMEM((8, WIDTH, 128), BF16),
            pltpu.VMEM((16, SIDE, WIDTH), BF16),
            pltpu.VMEM((2, 512, WIDE), BF16),
            pltpu.VMEM((2, 2, SIDE, 256), BF16),
            pltpu.VMEM((8, ROWS, 256), BF16),
            pltpu.VMEM((8, 288, 128), BF16),
            pltpu.VMEM((2, ROWS, 256), BF16),
            pltpu.VMEM((SLOTS, WIDTH, NSTATE), BF16),
            pltpu.VMEM((8, 128), jnp.int32),
            pltpu.VMEM((MOST, WIDTH, NSTATE), BF16),
            pltpu.VMEM((8, 128), jnp.int32),
            pltpu.VMEM((SLOTS, WIDTH, NSTATE), BF16),
            pltpu.VMEM((4, 8, 128), jnp.int32),
            pltpu.SMEM((4, 8, 128), jnp.int32),
            pltpu.SMEM((SLOTS,), jnp.int32),
            pltpu.VMEM((ROWS, WIDE), F32),
            pltpu.VMEM((ROWS, WIDE), BF16),
            pltpu.VMEM((ROWS, WIDE), BF16),
            pltpu.VMEM((SIDE, ROWS), BF16),
            pltpu.VMEM((SIDE, ROWS), BF16),
            pltpu.VMEM((MIXES, 640), BF16),
            pltpu.VMEM((8, MIXES, 640), BF16),
            pltpu.VMEM((128, 640), F32),
            pltpu.VMEM((640, NSTATE), BF16),
            pltpu.VMEM((640, NSTATE), BF16),
            pltpu.VMEM((640, 128), F32),
            pltpu.VMEM((2, ROWS, WIDTH), BF16),
            pltpu.VMEM((ROWS, 128), BF16),
        ]
        + [pltpu.VMEM((4, 4, 192, 256), BF16)] * 4
        + [dma((3, 4))] * 8
        + [dma((3, 16))] * 2
        + [dma((4, 3))] * 4
        + [dma((4,))] * 4
        + [dma((4,))] * 2
        + [dma((7,))] * 2
        + [dma((4,))] * 2
        + [dma((4, 4))] * 4
        + [dma] * 3
        + [dma((2,))] * 2,
        compiler_params=pltpu.CompilerParams(
            collective_id=0, has_side_effects=True, vmem_limit_bytes=58 * 1024 * 1024
        ),
        name="layer",
    )(moved, bias, rate, skip, win, wout, side, xmask, omask, xrows, kept, gain)


def on_device(
    frames_in,
    kept_state,
    moved_to,
    xz_weight,
    side_weight,
    xz_mask,
    dt_bias,
    decay_rate,
    skip_gain,
    norm_gain,
    out_weight,
    out_mask,
):
    mixed, carry = layer(
        moved_to,
        dt_bias,
        decay_rate,
        skip_gain,
        xz_weight,
        out_weight,
        side_weight,
        xz_mask,
        out_mask,
        frames_in.transpose(0, 2, 1, 3).reshape(QUARTER, FRAMES, WIDTH),
        kept_state.reshape(SLOTS, WIDTH, NSTATE),
        norm_gain,
    )
    return (
        mixed.reshape(SLOTS, TOKENS // FRAMES, FRAMES, WIDTH).transpose(0, 2, 1, 3),
        carry.reshape(SLOTS, 5, 64, NSTATE).astype(F32),
    )


def solution(mesh):
    placed = (
        P("stream", None, None, "shard"),
        P("stream", "shard", None, None),
        P("stream"),
        P("stream", None, "shard"),
        P("stream", None),
        P(),
        P("shard"),
        P("shard"),
        P("shard"),
        P("shard"),
        P("stream", "shard"),
        P(),
    )
    return jax.shard_map(
        on_device,
        mesh=mesh,
        in_specs=placed,
        out_specs=(P("stream", None, None, "shard"), P("stream", "shard", None, None)),
        check_vma=False,
    )
```
